32 devices in a mesh: member: 4 (over z), space: 8 (over y, x, core).
Axes of the slice: x: 2, y: 2, z: 4, core: 2. Of those that a mesh axis runs over, the one named last changes fastest.
Arguments:
- initial_ensemble: float32 [32, 6, 64, 512], P('member', None, 'space'), may hold values from -6 to 6
- obs_value: float32 [8, 2048], P('space'), may hold values from -6 to 6
- obs_error: float32 [8, 2048], P('space'), may hold values from 0.25 to 4
- obs_location: int32 [8, 2048], P('space'), may hold values from 0 to 24575, as said below
- patch_obs: int32 [8, 512, 64], P('space', 'member'), may hold values from 0 to 2047, as said below
- cotangent: float32 [32, 6, 64, 512], P('member', None, 'space'), may hold values from -6 to 6
Outputs:
- analysis: float32 [32, 6, 64, 512], P('member', None, 'space')
- gradient: float32 [32, 6, 64, 512], P('member', None, 'space')
The draws below stay inside these ranges and needn't reach their ends.
Inputs may be any that keep to these rules, and one draw needn't show every extreme that they name: `obs_location`: observation j of a tile lies in column (j * 512) // 2048; observation 0 lies at cell 0 and observation 2048 - 1 at cell 6 * 8 * 512 - 1. `patch_obs`: entry q of patch p is (((8 c + 3) * 2048) // 1024 + e) mod 2048 with c = p // 4 and -(32) <= e <= 32; entries may repeat.
All inputs are finite; a program needn't handle non-finite values.
Results may differ from the reference program's by a relative error of at most 0.0003.
Values sent between devices are 32-bit elements; how exact they have to be, the bound alone decides.
A program may use at most 192 MiB of HBM per device.

```python
import math
import jax
import jax.numpy as jnp
from jax import lax

FIELDS = 3
LEV = 2
STACK_QUANTITIES = 6
MEM_DEV = 8
SAMPLE_TOTAL = 32
SUBDOMAIN_HEIGHT = 8
MESH_WIDTH = 512
SUBDOMAIN_TOTAL = 8
MESH_HEIGHT = 64
NOBS = 2048
POBS = 64
PATCHES = 512
LOC_R = 8
NS_ITERS = 4
STEPS = 1


def draw_obs_location(key, part):
    key_var, key_row, key_col = jax.random.split(key, 3)
    obs_ids = jnp.arange(NOBS, dtype=jnp.int32)[None, :]
    variable = jax.random.randint(key_var, (SUBDOMAIN_TOTAL, NOBS), 0, STACK_QUANTITIES)
    row_pick = jax.random.randint(key_row, (SUBDOMAIN_TOTAL, NOBS), 0, SUBDOMAIN_HEIGHT)
    jitter = jax.random.randint(key_col, (SUBDOMAIN_TOTAL, NOBS), 0, max(MESH_WIDTH // NOBS, 1))
    column = obs_ids * MESH_WIDTH // NOBS + jitter
    flat_cell = variable * (SUBDOMAIN_HEIGHT * MESH_WIDTH) + row_pick * MESH_WIDTH + column
    flat_cell = jnp.where(obs_ids == 0, 0, flat_cell)
    flat_cell = jnp.where(obs_ids == NOBS - 1, STACK_QUANTITIES * SUBDOMAIN_HEIGHT * MESH_WIDTH - 1, flat_cell)
    return flat_cell.astype(jnp.int32)


def draw_patch_obs(key, part):
    patch_ids = jnp.arange(PATCHES, dtype=jnp.int32)[None, :, None]
    column_pair = patch_ids // (SUBDOMAIN_HEIGHT // 2)
    centre_obs = (8 * column_pair + 3) * NOBS // (2 * MESH_WIDTH)
    offsets = jax.random.randint(key, (SUBDOMAIN_TOTAL, PATCHES, POBS), -(POBS // 2), POBS // 2 + 1)
    return ((centre_obs + offsets) % NOBS).astype(jnp.int32)


def steps_of(key, extent, pieces, smallest, high):
    def one(axis_at, blocks):
        steps = jax.random.uniform(jax.random.fold_in(jax.random.fold_in(key, 6), axis_at), (blocks,), jnp.float32, smallest / len(pieces), high / len(pieces))
        return jnp.repeat(jnp.exp(steps), extent[axis_at] // blocks).reshape((-1,) + (1,) * (len(extent) - axis_at - 1))

    gain = one(*pieces[0])
    for cut in pieces[1:]:
        gain = gain * one(*cut)
    return gain


def centred(own_key, extent, scale, reach, pieces=(), kind=jnp.bfloat16):
    array = jax.random.normal(own_key, extent, jnp.float32) * scale
    if len(pieces) > 0:
        array = steps_of(own_key, extent, pieces, -0.22, 0.18) * array
    return jnp.clip(array, min=-reach, max=reach).astype(kind)


def setup_inputs(seed: int = 0) -> dict:
    splits = jax.random.split(jax.random.key(seed), 7)
    initial_ensemble = centred(splits[0], (SAMPLE_TOTAL, STACK_QUANTITIES, MESH_HEIGHT, MESH_WIDTH), 1.0, 6.0, ((0, 4), (2, 8)), jnp.float32)
    obs_value = centred(splits[1], (SUBDOMAIN_TOTAL, NOBS), 1.0, 6.0, ((0, 8),), jnp.float32)
    obs_error = jnp.clip(jnp.exp(math.log(4.0) - 2.7725887 * jax.random.uniform(splits[2], (SUBDOMAIN_TOTAL, NOBS), jnp.float32) ** steps_of(splits[2], (SUBDOMAIN_TOTAL, NOBS), ((0, 8),), -0.2, 0.2)), 0.25, 4.0)
    obs_location = draw_obs_location(jax.random.fold_in(splits[6], 71), 0)
    patch_obs = draw_patch_obs(jax.random.fold_in(splits[6], 71), 0)
    cotangent = centred(splits[5], (SAMPLE_TOTAL, STACK_QUANTITIES, MESH_HEIGHT, MESH_WIDTH), 1.0, 6.0, ((0, 4), (2, 8)), jnp.float32)
    return dict(initial_ensemble=initial_ensemble, obs_value=obs_value, obs_error=obs_error, obs_location=obs_location, patch_obs=patch_obs, cotangent=cotangent)


time_step = 0.2
coriolis = 0.5
stratification = 1.0
mixing = 0.3
highest = lax.Precision.HIGHEST

def row_diff(padded):
    return (padded[..., :-4, :] - 8.0 * padded[..., 1:-3, :] + 8.0 * padded[..., 3:-1, :] - padded[..., 4:, :]) / 12.0

def col_diff(field):
    return (jnp.roll(field, 2, axis=-1) - 8.0 * jnp.roll(field, 1, axis=-1) + 8.0 * jnp.roll(field, -1, axis=-1) - jnp.roll(field, -2, axis=-1)) / 12.0

def tendency(padded):
    members = padded.shape[0]
    layered = padded.reshape(members, FIELDS, LEV, padded.shape[2], padded.shape[3])
    interior = layered[:, :, :, 2:-2, :]
    along_rows = row_diff(layered)
    along_cols = col_diff(interior)
    speed_u = interior[:, 0]
    speed_v = interior[:, 1]
    carried = speed_u[:, None] * along_rows + speed_v[:, None] * along_cols
    rate_u = -carried[:, 0] + coriolis * speed_v - along_rows[:, 2]
    rate_v = -carried[:, 1] - coriolis * speed_u - along_cols[:, 2]
    rate_b = -carried[:, 2] - stratification * (along_rows[:, 0] + along_cols[:, 1])
    rates = jnp.stack([rate_u, rate_v, rate_b], axis=1)
    above = jnp.concatenate([interior[:, :, 1:], interior[:, :, -1:]], axis=2)
    below = jnp.concatenate([interior[:, :, :1], interior[:, :, :-1]], axis=2)
    rates = rates + mixing * (above - 2.0 * interior + below)
    return rates.reshape(members, FIELDS * LEV, interior.shape[3], interior.shape[4])

def wrap_rows(grid):
    return jnp.concatenate([grid[:, :, -2:], grid, grid[:, :, :2]], axis=2)

def propagate_dynamics(group):
    for step_count in range(STEPS):
        first_rate = tendency(wrap_rows(group))
        middle = group + time_step * first_rate
        second_rate = tendency(wrap_rows(middle))
        group = group + 0.5 * time_step * (first_rate + second_rate)
    return group

def analyse(ensemble, obs_ens, obs_values, obs_errors, obs_cells, patch_lists, first_col):
    members = ensemble.shape[0]
    variables = ensemble.shape[1]
    tile_rows = ensemble.shape[2]
    columns = ensemble.shape[3]
    half_rows = tile_rows // 2
    quads = columns // 4
    patch_count = half_rows * quads
    patch_ids = jnp.arange(patch_count, dtype=jnp.int32)
    patch_col = patch_ids // half_rows
    patch_row = patch_ids % half_rows
    picked = obs_ens[:, patch_lists]
    mean_obs = lax.optimization_barrier(jnp.mean(picked, axis=0))
    spread = picked - mean_obs
    innovation = obs_values[patch_lists] - mean_obs
    located = obs_cells[patch_lists]
    obs_row = located // MESH_WIDTH % SUBDOMAIN_HEIGHT
    obs_col = located % MESH_WIDTH
    row_gap = (obs_row - 2 * patch_row[:, None]).astype(jnp.float32) - 0.5
    col_shift = obs_col - 4 * (patch_col[:, None] + first_col // 4)
    col_shift = (col_shift + MESH_WIDTH // 2) % MESH_WIDTH - MESH_WIDTH // 2
    col_gap = col_shift.astype(jnp.float32) - 1.5
    weight = jnp.exp(-(row_gap * row_gap + col_gap * col_gap) / (2.0 * LOC_R * LOC_R)) / obs_errors[patch_lists]
    scaled = spread * weight
    identity = jnp.eye(members, dtype=jnp.float32)
    gram = (members - 1.0) * identity + jnp.einsum('kpq,jpq->pkj', scaled, spread, precision=highest)
    scale = jnp.sqrt(lax.optimization_barrier(jnp.sum(gram * gram, axis=(1, 2))))
    root_iter = gram / scale[:, None, None]
    inverse_root = jnp.broadcast_to(identity, gram.shape)
    for sweep in range(NS_ITERS):
        factor = 1.5 * identity - 0.5 * jnp.einsum('pij,pjk->pik', inverse_root, root_iter, precision=highest)
        root_iter = jnp.einsum('pij,pjk->pik', root_iter, factor, precision=highest)
        inverse_root = jnp.einsum('pij,pjk->pik', factor, inverse_root, precision=highest)
    forcing = jnp.einsum('kpq,pq->pk', scaled, innovation, precision=highest)
    half_way = jnp.einsum('pij,pj->pi', inverse_root, forcing, precision=highest)
    mean_weight = jnp.einsum('pij,pj->pi', inverse_root, half_way, precision=highest) / scale[:, None]
    weights = jnp.sqrt(members - 1.0) * inverse_root / jnp.sqrt(scale)[:, None, None] + mean_weight[:, :, None]
    patch_cells = ensemble.reshape(members, variables, half_rows, 2, quads, 4).transpose(4, 2, 0, 1, 3, 5)
    patch_cells = patch_cells.reshape(patch_count, members, variables * 8)
    centre = lax.optimization_barrier(jnp.mean(patch_cells, axis=1, keepdims=True))
    anomaly = patch_cells - centre
    updated = centre + jnp.einsum('pkc,pkj->pjc', anomaly, weights, precision=highest)
    updated = updated.reshape(quads, half_rows, members, variables, 2, 4).transpose(2, 3, 1, 4, 0, 5)
    return updated.reshape(members, variables, tile_rows, columns)

def reference(initial_ensemble, obs_value, obs_error, obs_location, patch_obs, cotangent):

    def whole(initial):
        subdomain_batches = initial.reshape(SAMPLE_TOTAL // MEM_DEV, MEM_DEV, STACK_QUANTITIES, MESH_HEIGHT, MESH_WIDTH)
        predicted_samples = lax.map(jax.checkpoint(propagate_dynamics), subdomain_batches).reshape(SAMPLE_TOTAL, STACK_QUANTITIES, MESH_HEIGHT, MESH_WIDTH)
        subdomain_slices = predicted_samples.reshape(SAMPLE_TOTAL, STACK_QUANTITIES, SUBDOMAIN_TOTAL, SUBDOMAIN_HEIGHT, MESH_WIDTH).transpose(2, 0, 1, 3, 4)

        def one_tile(inputs):
            tile_state, tile_values, tile_errors, tile_cells, tile_lists = inputs
            tile_obs = tile_state.reshape(SAMPLE_TOTAL, -1)[:, tile_cells]
            return analyse(tile_state, tile_obs, tile_values, tile_errors, tile_cells, tile_lists, 0)
        analysed = lax.map(jax.checkpoint(one_tile), (subdomain_slices, obs_value, obs_error, obs_location, patch_obs))
        return analysed.transpose(1, 2, 0, 3, 4).reshape(SAMPLE_TOTAL, STACK_QUANTITIES, MESH_HEIGHT, MESH_WIDTH)
    analysis, pullback = jax.vjp(whole, initial_ensemble)
    gradient = pullback(cotangent)[0]
    return (analysis, gradient)
```

```python
import jax
import jax.numpy as jnp
from jax import lax
from jax.experimental import pallas as pl
from jax.experimental.pallas import tpu as pltpu
from jax.sharding import PartitionSpec as P

FIELDS = 3
LEV = 2
SUBDOMAIN_HEIGHT = 8
MESH_WIDTH = 512
LOC_R = 8
NS_ITERS = 4
STEPS = 1


time_step = 0.2
coriolis = 0.5
stratification = 1.0
mixing = 0.3
highest = lax.Precision.HIGHEST


def padded_2(cells, sides, width):
    for axis, dim in sides:
        count = lax.axis_size(axis)
        head = lax.slice_in_dim(cells, 0, width, axis=dim)
        tail = lax.slice_in_dim(cells, cells.shape[dim] - width, cells.shape[dim], axis=dim)
        cells = jnp.concatenate(
            [
                lax.ppermute(tail, axis, [(i, (i + 1) % count) for i in range(count)]),
                cells,
                lax.ppermute(head, axis, [((i + 1) % count, i) for i in range(count)]),
            ],
            axis=dim,
        )
    return cells


def row_diff(padded):
    return (
        padded[..., :-4, :]
        - 8.0 * padded[..., 1:-3, :]
        + 8.0 * padded[..., 3:-1, :]
        - padded[..., 4:, :]
    ) / 12.0


def col_diff(field):
    return (
        jnp.roll(field, 2, axis=-1)
        - 8.0 * jnp.roll(field, 1, axis=-1)
        + 8.0 * jnp.roll(field, -1, axis=-1)
        - jnp.roll(field, -2, axis=-1)
    ) / 12.0


def tendency(padded):
    members = padded.shape[0]
    layered = padded.reshape(members, FIELDS, LEV, padded.shape[2], padded.shape[3])
    interior = layered[:, :, :, 2:-2, :]
    along_rows = row_diff(layered)
    along_cols = col_diff(interior)
    speed_u = interior[:, 0]
    speed_v = interior[:, 1]
    carried = speed_u[:, None] * along_rows + speed_v[:, None] * along_cols
    rate_u = -carried[:, 0] + coriolis * speed_v - along_rows[:, 2]
    rate_v = -carried[:, 1] - coriolis * speed_u - along_cols[:, 2]
    rate_b = -carried[:, 2] - stratification * (along_rows[:, 0] + along_cols[:, 1])
    rates = jnp.stack([rate_u, rate_v, rate_b], axis=1)
    above = jnp.concatenate([interior[:, :, 1:], interior[:, :, -1:]], axis=2)
    below = jnp.concatenate([interior[:, :, :1], interior[:, :, :-1]], axis=2)
    rates = rates + mixing * (above - 2.0 * interior + below)
    return rates.reshape(members, FIELDS * LEV, interior.shape[3], interior.shape[4])


def exchange_rims(edges):
    return padded_2(edges, (("space", 2),), 2)


def padded_rows(grid):
    edges = jnp.concatenate([grid[:, :, :2], grid[:, :, -2:]], axis=2)
    extended = exchange_rims(edges)
    return jnp.concatenate([extended[:, :, :2], grid, extended[:, :, -2:]], axis=2)


def return_rims(grad_padded):
    interior = grad_padded[:, :, 2:-2]
    edges = jnp.concatenate([grad_padded[:, :, :2], grad_padded[:, :, -2:]], axis=2)
    extended = exchange_rims(edges)
    interior = interior.at[:, :, :2].add(extended[:, :, :2])
    return interior.at[:, :, -2:].add(extended[:, :, -2:])


def analyse(ensemble, obs_ens, obs_values, obs_errors, obs_cells, patch_lists, first_col):
    members = ensemble.shape[0]
    variables = ensemble.shape[1]
    tile_rows = ensemble.shape[2]
    columns = ensemble.shape[3]
    half_rows = tile_rows // 2
    quads = columns // 4
    patch_count = half_rows * quads
    patch_ids = jnp.arange(patch_count, dtype=jnp.int32)
    patch_col = patch_ids // half_rows
    patch_row = patch_ids % half_rows
    picked = obs_ens[:, patch_lists]
    mean_obs = jnp.mean(picked, axis=0)
    spread = picked - mean_obs
    innovation = obs_values[patch_lists] - mean_obs
    located = obs_cells[patch_lists]
    obs_row = located // MESH_WIDTH % SUBDOMAIN_HEIGHT
    obs_col = located % MESH_WIDTH
    row_gap = (obs_row - 2 * patch_row[:, None]).astype(jnp.float32) - 0.5
    col_shift = obs_col - 4 * (patch_col[:, None] + first_col // 4)
    col_shift = (col_shift + MESH_WIDTH // 2) % MESH_WIDTH - MESH_WIDTH // 2
    col_gap = col_shift.astype(jnp.float32) - 1.5
    weight = (
        jnp.exp(-(row_gap * row_gap + col_gap * col_gap) / (2.0 * LOC_R * LOC_R))
        / obs_errors[patch_lists]
    )
    scaled = spread * weight
    identity = jnp.eye(members, dtype=jnp.float32)
    gram = (members - 1.0) * identity + jnp.einsum(
        "kpq,jpq->pkj", scaled, spread, precision=highest
    )
    scale = jnp.sqrt(jnp.sum(gram * gram, axis=(1, 2)))
    root_iter = gram / scale[:, None, None]
    inverse_root = jnp.broadcast_to(identity, gram.shape)
    for sweep in range(NS_ITERS):
        factor = 1.5 * identity - 0.5 * jnp.einsum(
            "pij,pjk->pik", inverse_root, root_iter, precision=highest
        )
        root_iter = jnp.einsum("pij,pjk->pik", root_iter, factor, precision=highest)
        inverse_root = jnp.einsum("pij,pjk->pik", factor, inverse_root, precision=highest)
    forcing = jnp.einsum("kpq,pq->pk", scaled, innovation, precision=highest)
    half_way = jnp.einsum("pij,pj->pi", inverse_root, forcing, precision=highest)
    mean_weight = (
        jnp.einsum("pij,pj->pi", inverse_root, half_way, precision=highest) / scale[:, None]
    )
    weights = (
        jnp.sqrt(members - 1.0) * inverse_root / jnp.sqrt(scale)[:, None, None]
        + mean_weight[:, :, None]
    )
    patch_cells = ensemble.reshape(members, variables, half_rows, 2, quads, 4).transpose(
        4, 2, 0, 1, 3, 5
    )
    patch_cells = patch_cells.reshape(patch_count, members, variables * 8)
    centre = jnp.mean(patch_cells, axis=1, keepdims=True)
    anomaly = patch_cells - centre
    updated = centre + jnp.einsum("pkc,pkj->pjc", anomaly, weights, precision=highest)
    updated = updated.reshape(quads, half_rows, members, variables, 2, 4).transpose(
        2, 3, 1, 4, 0, 5
    )
    return updated.reshape(members, variables, tile_rows, columns)


def owner_update(fore_owned, cot_owned, obs_ens, obs_values, obs_errors, obs_cells, patch_lists):
    columns = fore_owned.shape[3]
    width_block = min(32, columns)
    turn_count = columns // width_block
    patch_block = fore_owned.shape[2] // 2 * (width_block // 4)
    first_col = lax.axis_index("member") * columns

    def one_turn(obs_total, turn_index):
        col_start = turn_index * width_block
        fore_block = lax.dynamic_slice_in_dim(fore_owned, col_start, width_block, 3)
        cot_block = lax.dynamic_slice_in_dim(cot_owned, col_start, width_block, 3)
        list_block = lax.dynamic_slice_in_dim(patch_lists, turn_index * patch_block, patch_block, 0)

        def local_update(ensemble, observed):
            return analyse(
                ensemble,
                observed,
                obs_values,
                obs_errors,
                obs_cells,
                list_block,
                first_col + col_start,
            )

        updated, pullback = jax.vjp(local_update, fore_block, obs_ens)
        grad_block, grad_obs = pullback(cot_block)
        return (obs_total + grad_obs, (updated, grad_block))

    start_total = jnp.zeros(obs_ens.shape, jnp.float32)
    obs_total, stacked = lax.scan(one_turn, start_total, jnp.arange(turn_count, dtype=jnp.int32))
    updated_all = stacked[0].transpose(1, 2, 3, 0, 4).reshape(fore_owned.shape)
    grad_all = stacked[1].transpose(1, 2, 3, 0, 4).reshape(fore_owned.shape)
    return (updated_all, grad_all, obs_total)


def shards_wide(initial_ensemble, obs_value, obs_error, obs_location, patch_obs, cotangent):
    obs_values = obs_value[0]
    obs_errors = obs_error[0]
    obs_cells = obs_location[0]
    patch_lists = patch_obs[0]
    current = initial_ensemble
    step_count = 0
    first_pad = padded_rows(current)
    first_rate = tendency(first_pad)
    middle = current + time_step * first_rate
    second_pad = padded_rows(middle)
    second_rate = tendency(second_pad)
    trajectory = [(first_pad, second_pad)]
    current = current + 0.5 * time_step * (first_rate + second_rate)
    member_values = current.reshape(current.shape[0], -1)[:, obs_cells]
    obs_ens = lax.all_gather(member_values, "member", axis=0, tiled=True)
    fore_owned, cot_owned = (
        lax.all_to_all(current, "member", split_axis=3, concat_axis=0, tiled=True),
        lax.all_to_all(cotangent, "member", split_axis=3, concat_axis=0, tiled=True),
    )
    updated_owned, grad_owned, obs_total = owner_update(
        fore_owned, cot_owned, obs_ens, obs_values, obs_errors, obs_cells, patch_lists
    )
    analysis, grad_state = (
        lax.all_to_all(updated_owned, "member", split_axis=0, concat_axis=3, tiled=True),
        lax.all_to_all(grad_owned, "member", split_axis=0, concat_axis=3, tiled=True),
    )
    my_grad_obs = lax.psum_scatter(obs_total, "member", scatter_dimension=0, tiled=True)
    flat_grad = grad_state.reshape(grad_state.shape[0], -1).at[:, obs_cells].add(my_grad_obs)
    gradient = flat_grad.reshape(grad_state.shape)
    for step_count in reversed(range(STEPS)):
        first_pad, second_pad = trajectory[step_count]
        second_pull = jax.vjp(tendency, second_pad)[1]
        grad_middle = return_rims(second_pull(0.5 * time_step * gradient)[0])
        grad_first = 0.5 * time_step * gradient + time_step * grad_middle
        first_pull = jax.vjp(tendency, first_pad)[1]
        gradient = gradient + grad_middle + return_rims(first_pull(grad_first)[0])
    return (analysis, gradient)


LANES = 128
HALO = 8
OBS_PAD = 640


def dot_full(a, b, dims):
    return lax.dot_general(
        a, b, (dims, ((), ())), precision=highest, preferred_element_type=jnp.float32
    )


def analysis_kernel(x_ref, cot_ref, w_ref, val_ref, ana_ref, grad_ref, mats, cells, pairs, an, vecs, obs):
    members = x_ref.shape[0]
    variables = cot_ref.shape[1]
    norm = float(members - 1)
    square = members * members
    group = 4

    def patch_map(r):
        patch = lax.broadcasted_iota(jnp.int32, (LANES, LANES), 0)
        col = lax.broadcasted_iota(jnp.int32, (LANES, LANES), 1)
        hit = (patch // 4 == col // 4) & (patch % 4 == r)
        return jnp.where(hit, 1.0, 0.0).astype(jnp.float32)

    def rows_of(ref, i, size):
        return ref[pl.ds(pl.multiple_of(i * size, size), size), :]

    def eye_row(i):
        at = lax.broadcasted_iota(jnp.int32, (members, LANES), 0)
        return jnp.where(at == i, 1.0, 0.0).astype(jnp.float32)

    def product(out, terms, scale=1.0, shift=0.0):
        def body(block, carry):
            base = pl.multiple_of(block * (group * members), group * members)
            totals = [jnp.zeros((members, LANES), jnp.float32) for _ in range(group)]
            for k in range(members):
                for a, b in terms:
                    right = mats[b, k * members : (k + 1) * members, :]
                    for g in range(group):
                        left = mats[a, pl.ds(base + g * members + k, 1), :]
                        totals[g] = totals[g] + left * right
            for g in range(group):
                done = totals[g]
                if scale != 1.0:
                    done = scale * done
                if shift != 0.0:
                    done = done + shift * eye_row(block * group + g)
                mats[out, pl.ds(base + g * members, members), :] = done
            return carry

        lax.fori_loop(0, members // group, body, 0)

    def times_vec(m, slot):
        total = jnp.zeros((members, LANES), jnp.float32)
        for k in range(members):
            total = total + mats[m, k * members : (k + 1) * members, :] * vecs[slot, k : k + 1, :]
        return total

    xbar = lax.fori_loop(
        0, members, lambda k, t: t + x_ref[k, :variables], jnp.zeros((variables, 8, LANES), jnp.float32)
    ) * (1.0 / members)

    def centre(k, carry):
        an[k] = x_ref[k, :variables] - xbar
        return carry

    lax.fori_loop(0, members, centre, 0)

    def cell_pair(block, carry):
        held = [an[block * group + g] for g in range(group)]
        for j in range(members):
            cot = cot_ref[j]
            for g in range(group):
                at = pl.multiple_of((block * group + g) * members * 8, 8)
                cells[pl.ds(at + j * 8, 8), :] = jnp.sum(held[g] * cot, axis=0)
        return carry

    lax.fori_loop(0, members // group, cell_pair, 0)
    cot_weights = jnp.zeros((square, LANES), jnp.float32)
    for r in range(4):
        both = cells[pl.ds(2 * r, square, stride=8), :] + cells[pl.ds(2 * r + 1, square, stride=8), :]
        cot_weights = cot_weights + dot_full(both, patch_map(r), ((1,), (1,)))
    WB, B, M0, Y1, M1, Y2, Z2, M2, Y3, Z3, M3, Z4 = range(12)
    G, DM0, DY1, DM1, DY2, DZ2, DM2, DY3, DZ3, DM3, DZ4 = range(12, 23)
    mats[WB] = cot_weights

    for q in range(OBS_PAD // LANES):
        obs[:, q * LANES : (q + 1) * LANES] = x_ref[:, variables, q, :]
    seen = obs[...]
    seen_mean = jnp.sum(seen, axis=0, keepdims=True) * (1.0 / members)
    spread = seen - seen_mean
    obs[...] = spread
    innovation = val_ref[...] - seen_mean

    def outer(k, carry):
        pairs[pl.ds(pl.multiple_of(k * members, members), members), :] = obs[pl.ds(k, 1), :] * spread
        return carry

    lax.fori_loop(0, members, outer, 0)
    weight = w_ref[...]
    mats[B] = dot_full(pairs[...], weight, ((1,), (0,)))
    forcing = dot_full(spread * innovation, weight, ((1,), (0,)))

    def add_eye(i, total):
        row = mats[B, pl.ds(pl.multiple_of(i * members, members), members), :] + norm * eye_row(i)
        mats[B, pl.ds(pl.multiple_of(i * members, members), members), :] = row
        return total + row * row

    energy = lax.fori_loop(0, members, add_eye, jnp.zeros((members, LANES), jnp.float32))
    scale = jnp.sqrt(jnp.sum(energy, axis=0, keepdims=True))
    inv = 1.0 / scale

    def normalise(i, carry):
        at = pl.ds(pl.multiple_of(i * members, members), members)
        row = mats[B, at, :] * inv
        mats[B, at, :] = row
        mats[M0, at, :] = 1.5 * eye_row(i) - 0.5 * row
        return carry

    lax.fori_loop(0, members, normalise, 0)
    product(Y1, [(B, M0)])
    product(M1, [(M0, Y1)], -0.5, 1.5)
    product(Y2, [(Y1, M1)])
    product(Z2, [(M1, M0)])
    product(M2, [(Z2, Y2)], -0.5, 1.5)
    product(Y3, [(Y2, M2)])
    product(Z3, [(M2, Z2)])
    product(M3, [(Z3, Y3)], -0.5, 1.5)
    product(Z4, [(M3, Z3)])

    vecs[0] = forcing
    half = times_vec(Z4, 0)
    vecs[1] = half
    mean_weight = times_vec(Z4, 1) * inv
    vecs[2] = mean_weight
    root = jnp.sqrt(norm) / jnp.sqrt(scale)

    for r in range(4):
        spread_r = dot_full(
            (
                mats[Z4].reshape(members, members, LANES) * root[None]
                + mean_weight[:, None, :]
            ).reshape(square, LANES),
            patch_map(r),
            ((1,), (0,)),
        )
        cells[pl.ds(2 * r, square, stride=8), :] = spread_r
        cells[pl.ds(2 * r + 1, square, stride=8), :] = spread_r

    def update(block, carry):
        totals = [xbar for _ in range(group)]
        for k in range(members):
            piece = an[k]
            for g in range(group):
                at = pl.multiple_of((block * group + g) * 8, 8)
                totals[g] = totals[g] + piece * cells[pl.ds(at + k * members * 8, 8), :][None]
        for g in range(group):
            ana_ref[block * group + g] = totals[g]
        return carry

    lax.fori_loop(0, members // group, update, 0)

    def pull(block, carry):
        zero = jnp.zeros((variables, 8, LANES), jnp.float32)
        totals = [zero for _ in range(group)]
        for j in range(members):
            piece = cot_ref[j]
            for g in range(group):
                at = pl.multiple_of((block * group + g) * members * 8, 8)
                totals[g] = totals[g] + piece * cells[pl.ds(at + j * 8, 8), :][None]
        for g in range(group):
            grad_ref[block * group + g, :variables] = totals[g]
            carry = carry - totals[g]
        return carry

    short = lax.fori_loop(0, members // group, pull, jnp.zeros((variables, 8, LANES), jnp.float32))
    short = lax.fori_loop(0, members, lambda j, t: t + cot_ref[j], short) * (1.0 / members)

    def settle(k, carry):
        grad_ref[k, :variables] = grad_ref[k, :variables] + short
        return carry

    lax.fori_loop(0, members, settle, 0)

    cot_cube = mats[WB].reshape(members, members, LANES)
    mean_cot = jnp.sum(cot_cube, axis=1)
    vecs[3] = mean_cot
    half_cot = times_vec(Z4, 3) * inv
    vecs[4] = half_cot
    forcing_cot = times_vec(Z4, 4)
    overlap = jnp.sum(jnp.sum(mats[WB] * mats[Z4], axis=0, keepdims=True), axis=0, keepdims=True)
    scale_cot = (
        -0.5 * root * inv * overlap - jnp.sum(mean_cot * mean_weight, axis=0, keepdims=True) * inv
    )

    def symmetric(i, carry):
        at = pl.ds(pl.multiple_of(i * members, members), members)
        both = mats[WB, at, :] + mats[WB, pl.ds(i, members, stride=members), :]
        mean_i = vecs[3, pl.ds(i, 1), :]
        half_i = vecs[1, pl.ds(i, 1), :]
        half_cot_i = vecs[4, pl.ds(i, 1), :]
        forcing_i = vecs[0, pl.ds(i, 1), :]
        full = (0.5 * root) * both + 0.5 * (
            (mean_i * inv) * half
            + (half_i * inv) * mean_cot
            + half_cot_i * forcing
            + forcing_i * half_cot
        )
        mats[G, at, :] = full
        mats[DM0, at, :] = -0.5 * full
        return carry

    lax.fori_loop(0, members, symmetric, 0)
    product(DY1, [(G, M0), (B, DM0)])
    product(DM1, [(DM0, Y1), (M0, DY1)], -0.5)
    product(DY2, [(DY1, M1), (Y1, DM1)])
    product(DZ2, [(DM1, M0), (M1, DM0)])
    product(DM2, [(DZ2, Y2), (Z2, DY2)], -0.5)
    product(DY3, [(DY2, M2), (Y2, DM2)])
    product(DZ3, [(DM2, Z2), (M2, DZ2)])
    product(DM3, [(DZ3, Y3), (Z3, DY3)], -0.5)
    product(DZ4, [(DM3, Z3), (M3, DZ3)])
    scale_cot = scale_cot - jnp.sum(mats[DZ4] * mats[B], axis=0, keepdims=True) * inv
    gram_cot = mats[DZ4] * inv + scale_cot * mats[B]
    pairs[...] = dot_full(gram_cot, weight, ((1,), (1,)))
    scaled_cot = dot_full(forcing_cot, weight, ((1,), (1,)))
    seen_cot = scaled_cot * innovation

    def gather(j, total):
        block = pairs[pl.ds(pl.multiple_of(j * members, members), members), :]
        return total + block * obs[pl.ds(j, 1), :]

    seen_cot = seen_cot + 2.0 * lax.fori_loop(
        0, members, gather, jnp.zeros((members, OBS_PAD), jnp.float32)
    )
    innovation_cot = jnp.sum(scaled_cot * spread, axis=0, keepdims=True)
    mean_part = innovation_cot + jnp.sum(seen_cot, axis=0, keepdims=True)
    seen_cot = seen_cot - mean_part * (1.0 / members)
    for q in range(OBS_PAD // LANES):
        grad_ref[:, variables, q, :] = seen_cot[:, q * LANES : (q + 1) * LANES]
    for q in range(OBS_PAD // LANES, 8):
        grad_ref[:, variables, q, :] = jnp.zeros((members, LANES), jnp.float32)


def analysis_call(x, cot, weight, val):
    members = x.shape[0]
    square = members * members
    scratch = [
        pltpu.VMEM((23, square, LANES), jnp.float32),
        pltpu.VMEM((square * 8, LANES), jnp.float32),
        pltpu.VMEM((square, OBS_PAD), jnp.float32),
        pltpu.VMEM(cot.shape, jnp.float32),
        pltpu.VMEM((5, members, LANES), jnp.float32),
        pltpu.VMEM((members, OBS_PAD), jnp.float32),
    ]
    return pl.pallas_call(
        analysis_kernel,
        out_shape=(
            jax.ShapeDtypeStruct(cot.shape, jnp.float32),
            jax.ShapeDtypeStruct(x.shape, jnp.float32),
        ),
        in_specs=[pl.BlockSpec(memory_space=pltpu.VMEM)] * 4,
        out_specs=(pl.BlockSpec(memory_space=pltpu.VMEM),) * 2,
        scratch_shapes=scratch,
        compiler_params=pltpu.CompilerParams(vmem_limit_bytes=56 * 2**20),
    )(x, cot, weight, val)


def by_slot(flat, per_col):
    return flat.reshape(-1, per_col).T


def wrapped(rows):
    return jnp.concatenate([rows[..., -HALO:], rows, rows[..., :HALO]], axis=-1)


def obs_weights(obs_values, obs_errors, obs_cells, patch_lists, columns, tile_rows):
    nobs = obs_values.shape[0]
    per_col = nobs // MESH_WIDTH
    first_col = lax.axis_index("member") * columns
    span = columns + 2 * HALO

    def window(flat, fill):
        rows = wrapped(by_slot(flat, per_col))
        cut = lax.dynamic_slice_in_dim(rows, first_col, span, 1).reshape(-1)
        return jnp.pad(cut, (0, OBS_PAD - per_col * span), constant_values=fill)

    ids = window(jnp.arange(nobs, dtype=jnp.int32), -1)[:, None]
    located = window(obs_cells, 0)[:, None]
    errors = window(obs_errors, 1.0)[:, None]
    values = window(obs_values, 0.0)[None]
    half_rows = tile_rows // 2
    patch_ids = jnp.arange(patch_lists.shape[0], dtype=jnp.int32)[None]
    patch_col = patch_ids // half_rows
    patch_row = patch_ids % half_rows
    times = jnp.sum((patch_lists.T[:, None, :] == ids[None]).astype(jnp.float32), axis=0)
    obs_row = located // MESH_WIDTH % tile_rows
    obs_col = located % MESH_WIDTH
    row_gap = (obs_row - 2 * patch_row).astype(jnp.float32) - 0.5
    col_shift = obs_col - 4 * patch_col - first_col
    col_shift = (col_shift + MESH_WIDTH // 2) % MESH_WIDTH - MESH_WIDTH // 2
    col_gap = col_shift.astype(jnp.float32) - 1.5
    weight = times * (
        jnp.exp(-(row_gap * row_gap + col_gap * col_gap) / (2.0 * LOC_R * LOC_R)) / errors
    )
    return weight, values


def shards(initial_ensemble, obs_value, obs_error, obs_location, patch_obs, cotangent):
    obs_values = obs_value[0]
    obs_errors = obs_error[0]
    obs_cells = obs_location[0]
    patch_lists = patch_obs[0]
    count = lax.axis_size("member")
    local, variables, tile_rows, width = initial_ensemble.shape
    columns = width // count
    per_col = obs_cells.shape[0] // width
    span = columns + 2 * HALO
    stacked = variables * tile_rows

    def split(grid):
        return jnp.stack([grid[..., m * columns : (m + 1) * columns] for m in range(count)])

    def swap(blocks):
        return lax.all_to_all(blocks, "member", split_axis=0, concat_axis=0, tiled=True)

    def join(blocks):
        return jnp.concatenate([blocks[m] for m in range(count)], axis=-1)

    cot_owned = swap(split(cotangent)).reshape(count * local, variables, tile_rows, columns)
    weight, values = obs_weights(obs_values, obs_errors, obs_cells, patch_lists, columns, tile_rows)
    current = initial_ensemble
    first_pad = padded_rows(current)
    first_rate = tendency(first_pad)
    middle = current + time_step * first_rate
    second_pad = padded_rows(middle)
    second_rate = tendency(second_pad)
    current = current + 0.5 * time_step * (first_rate + second_rate)

    slot_cells = by_slot(obs_cells // width, per_col)
    level = jnp.arange(stacked, dtype=jnp.int32)[:, None]
    masks = [level == slot_cells[i][None] for i in range(per_col)]
    flat = current.reshape(local, stacked, width)
    seen = jnp.stack([jnp.sum(jnp.where(m, flat, 0.0), axis=1) for m in masks], axis=1)
    seen = wrapped(seen)
    seen = jnp.stack(
        [seen[..., m * columns : m * columns + span].reshape(local, per_col * span) for m in range(count)]
    )
    seen = jnp.pad(seen, ((0, 0), (0, 0), (0, tile_rows * LANES - per_col * span)))
    seen = seen.reshape(count, local, 1, tile_rows, LANES)
    payload = swap(jnp.concatenate([split(current), seen], axis=2))
    payload = payload.reshape(count * local, variables + 1, tile_rows, columns)
    ana_owned, grad_owned = analysis_call(payload, cot_owned, weight, values)
    analysis = join(swap(ana_owned.reshape(count, local, variables, tile_rows, columns)))
    back = swap(grad_owned.reshape(count, local, variables + 1, tile_rows, columns))
    grad_state = join(back[:, :, :variables])
    seen_back = back[:, :, variables].reshape(count, local, -1)[..., : per_col * span]
    seen_back = seen_back.reshape(count, local, per_col, span)
    total = sum(
        jnp.pad(seen_back[m], ((0, 0), (0, 0), (m * columns, width - columns - m * columns)))
        for m in range(count)
    )
    core = total[..., HALO:-HALO]
    head = total[..., -HALO:]
    tail = total[..., :HALO]
    core = core + jnp.concatenate(
        [head, jnp.zeros(core.shape[:-1] + (width - 2 * HALO,), jnp.float32), tail], axis=-1
    )
    gradient = grad_state.reshape(local, stacked, width)
    for i in range(per_col):
        gradient = gradient + jnp.where(masks[i], core[:, i][:, None], 0.0)
    gradient = gradient.reshape(initial_ensemble.shape)
    second_pull = jax.vjp(tendency, second_pad)[1]
    grad_middle = return_rims(second_pull(0.5 * time_step * gradient)[0])
    grad_first = 0.5 * time_step * gradient + time_step * grad_middle
    first_pull = jax.vjp(tendency, first_pad)[1]
    gradient = gradient + grad_middle + return_rims(first_pull(grad_first)[0])
    return (analysis, gradient)


def fits(initial_ensemble, obs_value, obs_error, obs_location, patch_obs, cotangent):
    members = initial_ensemble.shape[0] * lax.axis_size("member")
    width = initial_ensemble.shape[3]
    columns = width // lax.axis_size("member")
    nobs = obs_location.shape[1]
    return (
        members <= 32
        and columns == LANES
        and initial_ensemble.shape[2] == 8
        and nobs % width == 0
        and patch_obs.shape[2] // 2 <= 8 * nobs // width
        and nobs // width * (columns + 2 * HALO) <= OBS_PAD
    )


def chosen(*args):
    return shards(*args) if fits(*args) else shards_wide(*args)


def solution(mesh):
    placed = (
        P("member", None, "space", None),
        P("space", None),
        P("space", None),
        P("space", None),
        P("space", "member", None),
        P("member", None, "space", None),
    )
    return jax.shard_map(
        chosen,
        mesh=mesh,
        in_specs=placed,
        out_specs=(P("member", None, "space", None), P("member", None, "space", None)),
        check_vma=False,
    )
```

```python
import jax
import jax.numpy as jnp
from jax import lax
from jax.experimental import pallas as pl
from jax.experimental.pallas import tpu as pltpu
from jax.sharding import PartitionSpec as P

FIELDS = 3
LEV = 2
SUBDOMAIN_HEIGHT = 8
MESH_WIDTH = 512
LOC_R = 8
NS_ITERS = 4
STEPS = 1


time_step = 0.2
coriolis = 0.5
stratification = 1.0
mixing = 0.3
highest = lax.Precision.HIGHEST


def padded_2(cells, sides, width):
    for axis, dim in sides:
        count = lax.axis_size(axis)
        head = lax.slice_in_dim(cells, 0, width, axis=dim)
        tail = lax.slice_in_dim(cells, cells.shape[dim] - width, cells.shape[dim], axis=dim)
        cells = jnp.concatenate(
            [
                lax.ppermute(tail, axis, [(i, (i + 1) % count) for i in range(count)]),
                cells,
                lax.ppermute(head, axis, [((i + 1) % count, i) for i in range(count)]),
            ],
            axis=dim,
        )
    return cells


def row_diff(padded):
    return (
        padded[..., :-4, :]
        - 8.0 * padded[..., 1:-3, :]
        + 8.0 * padded[..., 3:-1, :]
        - padded[..., 4:, :]
    ) / 12.0


def col_diff(field):
    return (
        jnp.roll(field, 2, axis=-1)
        - 8.0 * jnp.roll(field, 1, axis=-1)
        + 8.0 * jnp.roll(field, -1, axis=-1)
        - jnp.roll(field, -2, axis=-1)
    ) / 12.0


def tendency(padded):
    members = padded.shape[0]
    layered = padded.reshape(members, FIELDS, LEV, padded.shape[2], padded.shape[3])
    interior = layered[:, :, :, 2:-2, :]
    along_rows = row_diff(layered)
    along_cols = col_diff(interior)
    speed_u = interior[:, 0]
    speed_v = interior[:, 1]
    carried = speed_u[:, None] * along_rows + speed_v[:, None] * along_cols
    rate_u = -carried[:, 0] + coriolis * speed_v - along_rows[:, 2]
    rate_v = -carried[:, 1] - coriolis * speed_u - along_cols[:, 2]
    rate_b = -carried[:, 2] - stratification * (along_rows[:, 0] + along_cols[:, 1])
    rates = jnp.stack([rate_u, rate_v, rate_b], axis=1)
    above = jnp.concatenate([interior[:, :, 1:], interior[:, :, -1:]], axis=2)
    below = jnp.concatenate([interior[:, :, :1], interior[:, :, :-1]], axis=2)
    rates = rates + mixing * (above - 2.0 * interior + below)
    return rates.reshape(members, FIELDS * LEV, interior.shape[3], interior.shape[4])


def exchange_rims(edges):
    return padded_2(edges, (("space", 2),), 2)


def padded_rows(grid):
    edges = jnp.concatenate([grid[:, :, :2], grid[:, :, -2:]], axis=2)
    extended = exchange_rims(edges)
    return jnp.concatenate([extended[:, :, :2], grid, extended[:, :, -2:]], axis=2)


def return_rims(grad_padded):
    interior = grad_padded[:, :, 2:-2]
    edges = jnp.concatenate([grad_padded[:, :, :2], grad_padded[:, :, -2:]], axis=2)
    extended = exchange_rims(edges)
    interior = interior.at[:, :, :2].add(extended[:, :, :2])
    return interior.at[:, :, -2:].add(extended[:, :, -2:])


def analyse(ensemble, obs_ens, obs_values, obs_errors, obs_cells, patch_lists, first_col):
    members = ensemble.shape[0]
    variables = ensemble.shape[1]
    tile_rows = ensemble.shape[2]
    columns = ensemble.shape[3]
    half_rows = tile_rows // 2
    quads = columns // 4
    patch_count = half_rows * quads
    patch_ids = jnp.arange(patch_count, dtype=jnp.int32)
    patch_col = patch_ids // half_rows
    patch_row = patch_ids % half_rows
    picked = obs_ens[:, patch_lists]
    mean_obs = jnp.mean(picked, axis=0)
    spread = picked - mean_obs
    innovation = obs_values[patch_lists] - mean_obs
    located = obs_cells[patch_lists]
    obs_row = located // MESH_WIDTH % SUBDOMAIN_HEIGHT
    obs_col = located % MESH_WIDTH
    row_gap = (obs_row - 2 * patch_row[:, None]).astype(jnp.float32) - 0.5
    col_shift = obs_col - 4 * (patch_col[:, None] + first_col // 4)
    col_shift = (col_shift + MESH_WIDTH // 2) % MESH_WIDTH - MESH_WIDTH // 2
    col_gap = col_shift.astype(jnp.float32) - 1.5
    weight = (
        jnp.exp(-(row_gap * row_gap + col_gap * col_gap) / (2.0 * LOC_R * LOC_R))
        / obs_errors[patch_lists]
    )
    scaled = spread * weight
    identity = jnp.eye(members, dtype=jnp.float32)
    gram = (members - 1.0) * identity + jnp.einsum(
        "kpq,jpq->pkj", scaled, spread, precision=highest
    )
    scale = jnp.sqrt(jnp.sum(gram * gram, axis=(1, 2)))
    root_iter = gram / scale[:, None, None]
    inverse_root = jnp.broadcast_to(identity, gram.shape)
    for sweep in range(NS_ITERS):
        factor = 1.5 * identity - 0.5 * jnp.einsum(
            "pij,pjk->pik", inverse_root, root_iter, precision=highest
        )
        root_iter = jnp.einsum("pij,pjk->pik", root_iter, factor, precision=highest)
        inverse_root = jnp.einsum("pij,pjk->pik", factor, inverse_root, precision=highest)
    forcing = jnp.einsum("kpq,pq->pk", scaled, innovation, precision=highest)
    half_way = jnp.einsum("pij,pj->pi", inverse_root, forcing, precision=highest)
    mean_weight = (
        jnp.einsum("pij,pj->pi", inverse_root, half_way, precision=highest) / scale[:, None]
    )
    weights = (
        jnp.sqrt(members - 1.0) * inverse_root / jnp.sqrt(scale)[:, None, None]
        + mean_weight[:, :, None]
    )
    patch_cells = ensemble.reshape(members, variables, half_rows, 2, quads, 4).transpose(
        4, 2, 0, 1, 3, 5
    )
    patch_cells = patch_cells.reshape(patch_count, members, variables * 8)
    centre = jnp.mean(patch_cells, axis=1, keepdims=True)
    anomaly = patch_cells - centre
    updated = centre + jnp.einsum("pkc,pkj->pjc", anomaly, weights, precision=highest)
    updated = updated.reshape(quads, half_rows, members, variables, 2, 4).transpose(
        2, 3, 1, 4, 0, 5
    )
    return updated.reshape(members, variables, tile_rows, columns)


def owner_update(fore_owned, cot_owned, obs_ens, obs_values, obs_errors, obs_cells, patch_lists):
    columns = fore_owned.shape[3]
    width_block = min(32, columns)
    turn_count = columns // width_block
    patch_block = fore_owned.shape[2] // 2 * (width_block // 4)
    first_col = lax.axis_index("member") * columns

    def one_turn(obs_total, turn_index):
        col_start = turn_index * width_block
        fore_block = lax.dynamic_slice_in_dim(fore_owned, col_start, width_block, 3)
        cot_block = lax.dynamic_slice_in_dim(cot_owned, col_start, width_block, 3)
        list_block = lax.dynamic_slice_in_dim(patch_lists, turn_index * patch_block, patch_block, 0)

        def local_update(ensemble, observed):
            return analyse(
                ensemble,
                observed,
                obs_values,
                obs_errors,
                obs_cells,
                list_block,
                first_col + col_start,
            )

        updated, pullback = jax.vjp(local_update, fore_block, obs_ens)
        grad_block, grad_obs = pullback(cot_block)
        return (obs_total + grad_obs, (updated, grad_block))

    start_total = jnp.zeros(obs_ens.shape, jnp.float32)
    obs_total, stacked = lax.scan(one_turn, start_total, jnp.arange(turn_count, dtype=jnp.int32))
    updated_all = stacked[0].transpose(1, 2, 3, 0, 4).reshape(fore_owned.shape)
    grad_all = stacked[1].transpose(1, 2, 3, 0, 4).reshape(fore_owned.shape)
    return (updated_all, grad_all, obs_total)


def shards_wide(initial_ensemble, obs_value, obs_error, obs_location, patch_obs, cotangent):
    obs_values = obs_value[0]
    obs_errors = obs_error[0]
    obs_cells = obs_location[0]
    patch_lists = patch_obs[0]
    current = initial_ensemble
    step_count = 0
    first_pad = padded_rows(current)
    first_rate = tendency(first_pad)
    middle = current + time_step * first_rate
    second_pad = padded_rows(middle)
    second_rate = tendency(second_pad)
    trajectory = [(first_pad, second_pad)]
    current = current + 0.5 * time_step * (first_rate + second_rate)
    member_values = current.reshape(current.shape[0], -1)[:, obs_cells]
    obs_ens = lax.all_gather(member_values, "member", axis=0, tiled=True)
    fore_owned, cot_owned = (
        lax.all_to_all(current, "member", split_axis=3, concat_axis=0, tiled=True),
        lax.all_to_all(cotangent, "member", split_axis=3, concat_axis=0, tiled=True),
    )
    updated_owned, grad_owned, obs_total = owner_update(
        fore_owned, cot_owned, obs_ens, obs_values, obs_errors, obs_cells, patch_lists
    )
    analysis, grad_state = (
        lax.all_to_all(updated_owned, "member", split_axis=0, concat_axis=3, tiled=True),
        lax.all_to_all(grad_owned, "member", split_axis=0, concat_axis=3, tiled=True),
    )
    my_grad_obs = lax.psum_scatter(obs_total, "member", scatter_dimension=0, tiled=True)
    flat_grad = grad_state.reshape(grad_state.shape[0], -1).at[:, obs_cells].add(my_grad_obs)
    gradient = flat_grad.reshape(grad_state.shape)
    for step_count in reversed(range(STEPS)):
        first_pad, second_pad = trajectory[step_count]
        second_pull = jax.vjp(tendency, second_pad)[1]
        grad_middle = return_rims(second_pull(0.5 * time_step * gradient)[0])
        grad_first = 0.5 * time_step * gradient + time_step * grad_middle
        first_pull = jax.vjp(tendency, first_pad)[1]
        gradient = gradient + grad_middle + return_rims(first_pull(grad_first)[0])
    return (analysis, gradient)


LANES = 128
HALO = 8
OBS_PAD = 640


def dot_full(a, b, dims):
    return lax.dot_general(
        a, b, (dims, ((), ())), precision=highest, preferred_element_type=jnp.float32
    )


def analysis_kernel(
    cur_ref, seen_ref, given_ref, w_ref, val_ref, ana_out, grad_out, seen_out,
    mats, cells, pairs, an, vecs, obs, x_ref, cot_ref, got_seen, ana_ref, grad_ref, part_ref,
    ana_got, grad_got, part_got, send_sem, recv_sem,
):
    members = x_ref.shape[0]
    variables = cot_ref.shape[1]
    count = lax.axis_size("member")
    local = members // count
    me = lax.axis_index("member")

    barrier = pltpu.get_barrier_semaphore()
    for s in range(1, count):
        pl.semaphore_signal(
            barrier,
            inc=1,
            device_id={"member": lax.rem(me + s, count)},
            device_id_type=pl.DeviceIdType.MESH,
        )
    pl.semaphore_wait(barrier, count - 1)

    def lanes(ref, m):
        return ref.at[:, :, :, pl.ds(pl.multiple_of(m * LANES, LANES), LANES)]

    def portion(ref, m):
        return ref.at[pl.ds(pl.multiple_of(m * local, local), local)]

    def send(stream, source, target):
        copies = []
        for s in range(1, count):
            peer = lax.rem(me + s, count)
            copy = pltpu.make_async_remote_copy(
                src_ref=source(peer),
                dst_ref=target,
                send_sem=send_sem.at[stream, s - 1],
                recv_sem=recv_sem.at[stream, s - 1],
                device_id={"member": peer},
                device_id_type=pl.DeviceIdType.MESH,
            )
            copy.start()
            copies.append(copy)
        return copies

    def arrive(copies):
        for copy in copies:
            copy.wait_recv()

    seen_sent = send(0, lambda m: seen_ref.at[m], portion(got_seen, me))
    cur_sent = send(1, lambda m: lanes(cur_ref, m), portion(x_ref, me))
    cot_sent = send(2, lambda m: lanes(given_ref, m), portion(cot_ref, me))
    mine = pl.ds(pl.multiple_of(me * local, local), local)
    own = pl.ds(pl.multiple_of(me * LANES, LANES), LANES)
    got_seen[mine] = seen_ref[me]
    x_ref[mine] = cur_ref[:, :, :, own]
    cot_ref[mine] = given_ref[:, :, :, own]
    norm = float(members - 1)
    square = members * members
    group = 4

    def patch_map(r):
        patch = lax.broadcasted_iota(jnp.int32, (LANES, LANES), 0)
        col = lax.broadcasted_iota(jnp.int32, (LANES, LANES), 1)
        hit = (patch // 4 == col // 4) & (patch % 4 == r)
        return jnp.where(hit, 1.0, 0.0).astype(jnp.float32)

    def rows_of(ref, i, size):
        return ref[pl.ds(pl.multiple_of(i * size, size), size), :]

    def eye_row(i):
        at = lax.broadcasted_iota(jnp.int32, (members, LANES), 0)
        return jnp.where(at == i, 1.0, 0.0).astype(jnp.float32)

    def product(out, terms, scale=1.0, shift=0.0):
        def body(block, carry):
            base = pl.multiple_of(block * (group * members), group * members)
            totals = [jnp.zeros((members, LANES), jnp.float32) for _ in range(group)]
            for k in range(members):
                for a, b in terms:
                    right = mats[b, k * members : (k + 1) * members, :]
                    for g in range(group):
                        left = mats[a, pl.ds(base + g * members + k, 1), :]
                        totals[g] = totals[g] + left * right
            for g in range(group):
                done = totals[g]
                if scale != 1.0:
                    done = scale * done
                if shift != 0.0:
                    done = done + shift * eye_row(block * group + g)
                mats[out, pl.ds(base + g * members, members), :] = done
            return carry

        lax.fori_loop(0, members // group, body, 0)

    def times_vec(m, slot):
        total = jnp.zeros((members, LANES), jnp.float32)
        for k in range(members):
            total = total + mats[m, k * members : (k + 1) * members, :] * vecs[slot, k : k + 1, :]
        return total

    WB, B, M0, Y1, M1, Y2, Z2, M2, Y3, Z3, M3, Z4 = range(12)
    G, DM0, DY1, DM1, DY2, DZ2, DM2, DY3, DZ3, DM3, DZ4 = range(12, 23)

    arrive(seen_sent)
    for q in range(OBS_PAD // LANES):
        obs[:, q * LANES : (q + 1) * LANES] = got_seen[:, q, :]
    seen = obs[...]
    seen_mean = jnp.sum(seen, axis=0, keepdims=True) * (1.0 / members)
    spread = seen - seen_mean
    obs[...] = spread
    innovation = val_ref[...] - seen_mean

    def outer(k, carry):
        pairs[pl.ds(pl.multiple_of(k * members, members), members), :] = obs[pl.ds(k, 1), :] * spread
        return carry

    lax.fori_loop(0, members, outer, 0)
    weight = w_ref[...]
    mats[B] = dot_full(pairs[...], weight, ((1,), (0,)))
    forcing = dot_full(spread * innovation, weight, ((1,), (0,)))

    def add_eye(i, total):
        row = mats[B, pl.ds(pl.multiple_of(i * members, members), members), :] + norm * eye_row(i)
        mats[B, pl.ds(pl.multiple_of(i * members, members), members), :] = row
        return total + row * row

    energy = lax.fori_loop(0, members, add_eye, jnp.zeros((members, LANES), jnp.float32))
    scale = jnp.sqrt(jnp.sum(energy, axis=0, keepdims=True))
    inv = 1.0 / scale

    def normalise(i, carry):
        at = pl.ds(pl.multiple_of(i * members, members), members)
        row = mats[B, at, :] * inv
        mats[B, at, :] = row
        mats[M0, at, :] = 1.5 * eye_row(i) - 0.5 * row
        return carry

    lax.fori_loop(0, members, normalise, 0)
    product(Y1, [(B, M0)])
    product(M1, [(M0, Y1)], -0.5, 1.5)
    product(Y2, [(Y1, M1)])
    product(Z2, [(M1, M0)])
    product(M2, [(Z2, Y2)], -0.5, 1.5)
    product(Y3, [(Y2, M2)])
    product(Z3, [(M2, Z2)])
    product(M3, [(Z3, Y3)], -0.5, 1.5)
    product(Z4, [(M3, Z3)])

    vecs[0] = forcing
    half = times_vec(Z4, 0)
    vecs[1] = half
    mean_weight = times_vec(Z4, 1) * inv
    vecs[2] = mean_weight
    root = jnp.sqrt(norm) / jnp.sqrt(scale)

    arrive(cur_sent)
    xbar = lax.fori_loop(
        0, members, lambda k, t: t + x_ref[k], jnp.zeros((variables, 8, LANES), jnp.float32)
    ) * (1.0 / members)

    def centre(k, carry):
        an[k] = x_ref[k] - xbar
        return carry

    lax.fori_loop(0, members, centre, 0)

    for r in range(4):
        spread_r = dot_full(
            (
                mats[Z4].reshape(members, members, LANES) * root[None]
                + mean_weight[:, None, :]
            ).reshape(square, LANES),
            patch_map(r),
            ((1,), (0,)),
        )
        cells[pl.ds(2 * r, square, stride=8), :] = spread_r
        cells[pl.ds(2 * r + 1, square, stride=8), :] = spread_r

    def update(block, carry):
        totals = [xbar for _ in range(group)]
        for k in range(members):
            piece = an[k]
            for g in range(group):
                at = pl.multiple_of((block * group + g) * 8, 8)
                totals[g] = totals[g] + piece * cells[pl.ds(at + k * members * 8, 8), :][None]
        for g in range(group):
            ana_ref[block * group + g] = totals[g]
        return carry

    lax.fori_loop(0, members // group, update, 0)

    ana_sent = send(3, lambda m: portion(ana_ref, m), portion(ana_got, me))
    arrive(cot_sent)

    def pull(block, carry):
        zero = jnp.zeros((variables, 8, LANES), jnp.float32)
        totals = [zero for _ in range(group)]
        for j in range(members):
            piece = cot_ref[j]
            for g in range(group):
                at = pl.multiple_of((block * group + g) * members * 8, 8)
                totals[g] = totals[g] + piece * cells[pl.ds(at + j * 8, 8), :][None]
        for g in range(group):
            grad_ref[block * group + g] = totals[g]
            carry = carry - totals[g]
        return carry

    short = lax.fori_loop(0, members // group, pull, jnp.zeros((variables, 8, LANES), jnp.float32))
    short = lax.fori_loop(0, members, lambda j, t: t + cot_ref[j], short) * (1.0 / members)

    def settle(k, carry):
        grad_ref[k] = grad_ref[k] + short
        return carry

    lax.fori_loop(0, members, settle, 0)

    grad_sent = send(4, lambda m: portion(grad_ref, m), portion(grad_got, me))

    def cell_pair(block, carry):
        held = [an[block * group + g] for g in range(group)]
        for j in range(members):
            cot = cot_ref[j]
            for g in range(group):
                at = pl.multiple_of((block * group + g) * members * 8, 8)
                cells[pl.ds(at + j * 8, 8), :] = jnp.sum(held[g] * cot, axis=0)
        return carry

    lax.fori_loop(0, members // group, cell_pair, 0)
    cot_weights = jnp.zeros((square, LANES), jnp.float32)
    for r in range(4):
        both = cells[pl.ds(2 * r, square, stride=8), :] + cells[pl.ds(2 * r + 1, square, stride=8), :]
        cot_weights = cot_weights + dot_full(both, patch_map(r), ((1,), (1,)))
    mats[WB] = cot_weights

    cot_cube = mats[WB].reshape(members, members, LANES)
    mean_cot = jnp.sum(cot_cube, axis=1)
    vecs[3] = mean_cot
    half_cot = times_vec(Z4, 3) * inv
    vecs[4] = half_cot
    forcing_cot = times_vec(Z4, 4)
    overlap = jnp.sum(jnp.sum(mats[WB] * mats[Z4], axis=0, keepdims=True), axis=0, keepdims=True)
    scale_cot = (
        -0.5 * root * inv * overlap - jnp.sum(mean_cot * mean_weight, axis=0, keepdims=True) * inv
    )

    def symmetric(i, carry):
        at = pl.ds(pl.multiple_of(i * members, members), members)
        both = mats[WB, at, :] + mats[WB, pl.ds(i, members, stride=members), :]
        mean_i = vecs[3, pl.ds(i, 1), :]
        half_i = vecs[1, pl.ds(i, 1), :]
        half_cot_i = vecs[4, pl.ds(i, 1), :]
        forcing_i = vecs[0, pl.ds(i, 1), :]
        full = (0.5 * root) * both + 0.5 * (
            (mean_i * inv) * half
            + (half_i * inv) * mean_cot
            + half_cot_i * forcing
            + forcing_i * half_cot
        )
        mats[G, at, :] = full
        mats[DM0, at, :] = -0.5 * full
        return carry

    lax.fori_loop(0, members, symmetric, 0)
    product(DY1, [(G, M0), (B, DM0)])
    product(DM1, [(DM0, Y1), (M0, DY1)], -0.5)
    product(DY2, [(DY1, M1), (Y1, DM1)])
    product(DZ2, [(DM1, M0), (M1, DM0)])
    product(DM2, [(DZ2, Y2), (Z2, DY2)], -0.5)
    product(DY3, [(DY2, M2), (Y2, DM2)])
    product(DZ3, [(DM2, Z2), (M2, DZ2)])
    product(DM3, [(DZ3, Y3), (Z3, DY3)], -0.5)
    product(DZ4, [(DM3, Z3), (M3, DZ3)])
    scale_cot = scale_cot - jnp.sum(mats[DZ4] * mats[B], axis=0, keepdims=True) * inv
    gram_cot = mats[DZ4] * inv + scale_cot * mats[B]
    pairs[...] = dot_full(gram_cot, weight, ((1,), (1,)))
    scaled_cot = dot_full(forcing_cot, weight, ((1,), (1,)))
    seen_cot = scaled_cot * innovation

    def gather(j, total):
        block = pairs[pl.ds(pl.multiple_of(j * members, members), members), :]
        return total + block * obs[pl.ds(j, 1), :]

    seen_cot = seen_cot + 2.0 * lax.fori_loop(
        0, members, gather, jnp.zeros((members, OBS_PAD), jnp.float32)
    )
    innovation_cot = jnp.sum(scaled_cot * spread, axis=0, keepdims=True)
    mean_part = innovation_cot + jnp.sum(seen_cot, axis=0, keepdims=True)
    seen_cot = seen_cot - mean_part * (1.0 / members)
    for q in range(OBS_PAD // LANES):
        part_ref[:, q, :] = seen_cot[:, q * LANES : (q + 1) * LANES]
    for q in range(OBS_PAD // LANES, 8):
        part_ref[:, q, :] = jnp.zeros((members, LANES), jnp.float32)
    part_sent = send(5, lambda m: portion(part_ref, m), portion(part_got, me))
    ana_got[mine] = ana_ref[mine]
    grad_got[mine] = grad_ref[mine]
    part_got[mine] = part_ref[mine]
    arrive(ana_sent)
    arrive(grad_sent)
    for m in range(count):
        cut = slice(m * local, (m + 1) * local)
        ana_out[:, :, :, m * LANES : (m + 1) * LANES] = ana_got[cut]
        grad_out[:, :, :, m * LANES : (m + 1) * LANES] = grad_got[cut]
    arrive(part_sent)
    for m in range(count):
        seen_out[m] = part_got[m * local : (m + 1) * local]
    for copies in (seen_sent, cur_sent, cot_sent, ana_sent, grad_sent, part_sent):
        for copy in copies:
            copy.wait_send()


def analysis_call(current, seen, cotangent, weight, val):
    count = seen.shape[0]
    local, variables = current.shape[:2]
    members = count * local
    square = members * members
    whole = pltpu.VMEM((members, variables, 8, LANES), jnp.float32)
    small = pltpu.VMEM((members, 8, LANES), jnp.float32)
    scratch = [
        pltpu.VMEM((23, square, LANES), jnp.float32),
        pltpu.VMEM((square * 8, LANES), jnp.float32),
        pltpu.VMEM((square, OBS_PAD), jnp.float32),
        whole,
        pltpu.VMEM((5, members, LANES), jnp.float32),
        pltpu.VMEM((members, OBS_PAD), jnp.float32),
        whole,
        whole,
        small,
        whole,
        whole,
        small,
        whole,
        whole,
        small,
        pltpu.SemaphoreType.DMA((6, count - 1)),
        pltpu.SemaphoreType.DMA((6, count - 1)),
    ]
    return pl.pallas_call(
        analysis_kernel,
        out_shape=(
            jax.ShapeDtypeStruct(current.shape, jnp.float32),
            jax.ShapeDtypeStruct(current.shape, jnp.float32),
            jax.ShapeDtypeStruct(seen.shape, jnp.float32),
        ),
        in_specs=[pl.BlockSpec(memory_space=pltpu.VMEM)] * 5,
        out_specs=(pl.BlockSpec(memory_space=pltpu.VMEM),) * 3,
        scratch_shapes=scratch,
        compiler_params=pltpu.CompilerParams(
            vmem_limit_bytes=56 * 2**20, collective_id=0, has_side_effects=True
        ),
    )(current, seen, cotangent, weight, val)


def by_slot(flat, per_col):
    return flat.reshape(-1, per_col).T


def wrapped(rows):
    return jnp.concatenate([rows[..., -HALO:], rows, rows[..., :HALO]], axis=-1)


def obs_weights(obs_values, obs_errors, obs_cells, patch_lists, columns, tile_rows):
    nobs = obs_values.shape[0]
    per_col = nobs // MESH_WIDTH
    first_col = lax.axis_index("member") * columns
    span = columns + 2 * HALO

    def window(flat, fill):
        rows = wrapped(by_slot(flat, per_col))
        cut = lax.dynamic_slice_in_dim(rows, first_col, span, 1).reshape(-1)
        return jnp.pad(cut, (0, OBS_PAD - per_col * span), constant_values=fill)

    ids = window(jnp.arange(nobs, dtype=jnp.int32), -1)[:, None]
    located = window(obs_cells, 0)[:, None]
    errors = window(obs_errors, 1.0)[:, None]
    values = window(obs_values, 0.0)[None]
    half_rows = tile_rows // 2
    patch_ids = jnp.arange(patch_lists.shape[0], dtype=jnp.int32)[None]
    patch_col = patch_ids // half_rows
    patch_row = patch_ids % half_rows
    times = jnp.sum((patch_lists.T[:, None, :] == ids[None]).astype(jnp.float32), axis=0)
    obs_row = located // MESH_WIDTH % tile_rows
    obs_col = located % MESH_WIDTH
    row_gap = (obs_row - 2 * patch_row).astype(jnp.float32) - 0.5
    col_shift = obs_col - 4 * patch_col - first_col
    col_shift = (col_shift + MESH_WIDTH // 2) % MESH_WIDTH - MESH_WIDTH // 2
    col_gap = col_shift.astype(jnp.float32) - 1.5
    weight = times * (
        jnp.exp(-(row_gap * row_gap + col_gap * col_gap) / (2.0 * LOC_R * LOC_R)) / errors
    )
    return weight, values


def shards(initial_ensemble, obs_value, obs_error, obs_location, patch_obs, cotangent):
    obs_values = obs_value[0]
    obs_errors = obs_error[0]
    obs_cells = obs_location[0]
    patch_lists = patch_obs[0]
    count = lax.axis_size("member")
    local, variables, tile_rows, width = initial_ensemble.shape
    columns = width // count
    per_col = obs_cells.shape[0] // width
    span = columns + 2 * HALO
    stacked = variables * tile_rows

    weight, values = obs_weights(obs_values, obs_errors, obs_cells, patch_lists, columns, tile_rows)
    current = initial_ensemble
    first_pad = padded_rows(current)
    first_rate = tendency(first_pad)
    middle = current + time_step * first_rate
    second_pad = padded_rows(middle)
    second_rate = tendency(second_pad)
    current = current + 0.5 * time_step * (first_rate + second_rate)

    slot_cells = by_slot(obs_cells // width, per_col)
    level = jnp.arange(stacked, dtype=jnp.int32)[:, None]
    masks = [level == slot_cells[i][None] for i in range(per_col)]
    flat = current.reshape(local, stacked, width)
    seen = jnp.stack([jnp.sum(jnp.where(m, flat, 0.0), axis=1) for m in masks], axis=1)
    seen = wrapped(seen)
    seen = jnp.stack(
        [seen[..., m * columns : m * columns + span].reshape(local, per_col * span) for m in range(count)]
    )
    seen = jnp.pad(seen, ((0, 0), (0, 0), (0, tile_rows * LANES - per_col * span)))
    seen = seen.reshape(count, local, tile_rows, LANES)
    analysis, grad_state, back = analysis_call(current, seen, cotangent, weight, values)
    seen_back = back.reshape(count, local, -1)[..., : per_col * span]
    seen_back = seen_back.reshape(count, local, per_col, span)
    total = sum(
        jnp.pad(seen_back[m], ((0, 0), (0, 0), (m * columns, width - columns - m * columns)))
        for m in range(count)
    )
    core = total[..., HALO:-HALO]
    head = total[..., -HALO:]
    tail = total[..., :HALO]
    core = core + jnp.concatenate(
        [head, jnp.zeros(core.shape[:-1] + (width - 2 * HALO,), jnp.float32), tail], axis=-1
    )
    gradient = grad_state.reshape(local, stacked, width)
    for i in range(per_col):
        gradient = gradient + jnp.where(masks[i], core[:, i][:, None], 0.0)
    gradient = gradient.reshape(initial_ensemble.shape)
    second_pull = jax.vjp(tendency, second_pad)[1]
    grad_middle = return_rims(second_pull(0.5 * time_step * gradient)[0])
    grad_first = 0.5 * time_step * gradient + time_step * grad_middle
    first_pull = jax.vjp(tendency, first_pad)[1]
    gradient = gradient + grad_middle + return_rims(first_pull(grad_first)[0])
    return (analysis, gradient)


def fits(initial_ensemble, obs_value, obs_error, obs_location, patch_obs, cotangent):
    members = initial_ensemble.shape[0] * lax.axis_size("member")
    width = initial_ensemble.shape[3]
    columns = width // lax.axis_size("member")
    nobs = obs_location.shape[1]
    return (
        members <= 32
        and columns == LANES
        and initial_ensemble.shape[2] == 8
        and nobs % width == 0
        and patch_obs.shape[2] // 2 <= 8 * nobs // width
        and nobs // width * (columns + 2 * HALO) <= OBS_PAD
    )


def chosen(*args):
    return shards(*args) if fits(*args) else shards_wide(*args)


def solution(mesh):
    placed = (
        P("member", None, "space", None),
        P("space", None),
        P("space", None),
        P("space", None),
        P("space", "member", None),
        P("member", None, "space", None),
    )
    return jax.shard_map(
        chosen,
        mesh=mesh,
        in_specs=placed,
        out_specs=(P("member", None, "space", None), P("member", None, "space", None)),
        check_vma=False,
    )
```

```python
import jax
import jax.numpy as jnp
from jax import lax
from jax.experimental import pallas as pl
from jax.experimental.pallas import tpu as pltpu
from jax.sharding import PartitionSpec as P

FIELDS = 3
LEV = 2
SUBDOMAIN_HEIGHT = 8
MESH_WIDTH = 512
LOC_R = 8
NS_ITERS = 4
STEPS = 1


time_step = 0.2
coriolis = 0.5
stratification = 1.0
mixing = 0.3
highest = lax.Precision.HIGHEST


def padded_2(cells, sides, width):
    for axis, dim in sides:
        count = lax.axis_size(axis)
        head = lax.slice_in_dim(cells, 0, width, axis=dim)
        tail = lax.slice_in_dim(cells, cells.shape[dim] - width, cells.shape[dim], axis=dim)
        cells = jnp.concatenate(
            [
                lax.ppermute(tail, axis, [(i, (i + 1) % count) for i in range(count)]),
                cells,
                lax.ppermute(head, axis, [((i + 1) % count, i) for i in range(count)]),
            ],
            axis=dim,
        )
    return cells


def row_diff(padded):
    return (
        padded[..., :-4, :]
        - 8.0 * padded[..., 1:-3, :]
        + 8.0 * padded[..., 3:-1, :]
        - padded[..., 4:, :]
    ) / 12.0


def col_diff(field):
    return (
        jnp.roll(field, 2, axis=-1)
        - 8.0 * jnp.roll(field, 1, axis=-1)
        + 8.0 * jnp.roll(field, -1, axis=-1)
        - jnp.roll(field, -2, axis=-1)
    ) / 12.0


def tendency(padded):
    members = padded.shape[0]
    layered = padded.reshape(members, FIELDS, LEV, padded.shape[2], padded.shape[3])
    interior = layered[:, :, :, 2:-2, :]
    along_rows = row_diff(layered)
    along_cols = col_diff(interior)
    speed_u = interior[:, 0]
    speed_v = interior[:, 1]
    carried = speed_u[:, None] * along_rows + speed_v[:, None] * along_cols
    rate_u = -carried[:, 0] + coriolis * speed_v - along_rows[:, 2]
    rate_v = -carried[:, 1] - coriolis * speed_u - along_cols[:, 2]
    rate_b = -carried[:, 2] - stratification * (along_rows[:, 0] + along_cols[:, 1])
    rates = jnp.stack([rate_u, rate_v, rate_b], axis=1)
    above = jnp.concatenate([interior[:, :, 1:], interior[:, :, -1:]], axis=2)
    below = jnp.concatenate([interior[:, :, :1], interior[:, :, :-1]], axis=2)
    rates = rates + mixing * (above - 2.0 * interior + below)
    return rates.reshape(members, FIELDS * LEV, interior.shape[3], interior.shape[4])


def exchange_rims(edges):
    return padded_2(edges, (("space", 2),), 2)


def padded_rows(grid):
    edges = jnp.concatenate([grid[:, :, :2], grid[:, :, -2:]], axis=2)
    extended = exchange_rims(edges)
    return jnp.concatenate([extended[:, :, :2], grid, extended[:, :, -2:]], axis=2)


def return_rims(grad_padded):
    interior = grad_padded[:, :, 2:-2]
    edges = jnp.concatenate([grad_padded[:, :, :2], grad_padded[:, :, -2:]], axis=2)
    extended = exchange_rims(edges)
    interior = interior.at[:, :, :2].add(extended[:, :, :2])
    return interior.at[:, :, -2:].add(extended[:, :, -2:])


def analyse(ensemble, obs_ens, obs_values, obs_errors, obs_cells, patch_lists, first_col):
    members = ensemble.shape[0]
    variables = ensemble.shape[1]
    tile_rows = ensemble.shape[2]
    columns = ensemble.shape[3]
    half_rows = tile_rows // 2
    quads = columns // 4
    patch_count = half_rows * quads
    patch_ids = jnp.arange(patch_count, dtype=jnp.int32)
    patch_col = patch_ids // half_rows
    patch_row = patch_ids % half_rows
    picked = obs_ens[:, patch_lists]
    mean_obs = jnp.mean(picked, axis=0)
    spread = picked - mean_obs
    innovation = obs_values[patch_lists] - mean_obs
    located = obs_cells[patch_lists]
    obs_row = located // MESH_WIDTH % SUBDOMAIN_HEIGHT
    obs_col = located % MESH_WIDTH
    row_gap = (obs_row - 2 * patch_row[:, None]).astype(jnp.float32) - 0.5
    col_shift = obs_col - 4 * (patch_col[:, None] + first_col // 4)
    col_shift = (col_shift + MESH_WIDTH // 2) % MESH_WIDTH - MESH_WIDTH // 2
    col_gap = col_shift.astype(jnp.float32) - 1.5
    weight = (
        jnp.exp(-(row_gap * row_gap + col_gap * col_gap) / (2.0 * LOC_R * LOC_R))
        / obs_errors[patch_lists]
    )
    scaled = spread * weight
    identity = jnp.eye(members, dtype=jnp.float32)
    gram = (members - 1.0) * identity + jnp.einsum(
        "kpq,jpq->pkj", scaled, spread, precision=highest
    )
    scale = jnp.sqrt(jnp.sum(gram * gram, axis=(1, 2)))
    root_iter = gram / scale[:, None, None]
    inverse_root = jnp.broadcast_to(identity, gram.shape)
    for sweep in range(NS_ITERS):
        factor = 1.5 * identity - 0.5 * jnp.einsum(
            "pij,pjk->pik", inverse_root, root_iter, precision=highest
        )
        root_iter = jnp.einsum("pij,pjk->pik", root_iter, factor, precision=highest)
        inverse_root = jnp.einsum("pij,pjk->pik", factor, inverse_root, precision=highest)
    forcing = jnp.einsum("kpq,pq->pk", scaled, innovation, precision=highest)
    half_way = jnp.einsum("pij,pj->pi", inverse_root, forcing, precision=highest)
    mean_weight = (
        jnp.einsum("pij,pj->pi", inverse_root, half_way, precision=highest) / scale[:, None]
    )
    weights = (
        jnp.sqrt(members - 1.0) * inverse_root / jnp.sqrt(scale)[:, None, None]
        + mean_weight[:, :, None]
    )
    patch_cells = ensemble.reshape(members, variables, half_rows, 2, quads, 4).transpose(
        4, 2, 0, 1, 3, 5
    )
    patch_cells = patch_cells.reshape(patch_count, members, variables * 8)
    centre = jnp.mean(patch_cells, axis=1, keepdims=True)
    anomaly = patch_cells - centre
    updated = centre + jnp.einsum("pkc,pkj->pjc", anomaly, weights, precision=highest)
    updated = updated.reshape(quads, half_rows, members, variables, 2, 4).transpose(
        2, 3, 1, 4, 0, 5
    )
    return updated.reshape(members, variables, tile_rows, columns)


def owner_update(fore_owned, cot_owned, obs_ens, obs_values, obs_errors, obs_cells, patch_lists):
    columns = fore_owned.shape[3]
    width_block = min(32, columns)
    turn_count = columns // width_block
    patch_block = fore_owned.shape[2] // 2 * (width_block // 4)
    first_col = lax.axis_index("member") * columns

    def one_turn(obs_total, turn_index):
        col_start = turn_index * width_block
        fore_block = lax.dynamic_slice_in_dim(fore_owned, col_start, width_block, 3)
        cot_block = lax.dynamic_slice_in_dim(cot_owned, col_start, width_block, 3)
        list_block = lax.dynamic_slice_in_dim(patch_lists, turn_index * patch_block, patch_block, 0)

        def local_update(ensemble, observed):
            return analyse(
                ensemble,
                observed,
                obs_values,
                obs_errors,
                obs_cells,
                list_block,
                first_col + col_start,
            )

        updated, pullback = jax.vjp(local_update, fore_block, obs_ens)
        grad_block, grad_obs = pullback(cot_block)
        return (obs_total + grad_obs, (updated, grad_block))

    start_total = jnp.zeros(obs_ens.shape, jnp.float32)
    obs_total, stacked = lax.scan(one_turn, start_total, jnp.arange(turn_count, dtype=jnp.int32))
    updated_all = stacked[0].transpose(1, 2, 3, 0, 4).reshape(fore_owned.shape)
    grad_all = stacked[1].transpose(1, 2, 3, 0, 4).reshape(fore_owned.shape)
    return (updated_all, grad_all, obs_total)


def shards_wide(initial_ensemble, obs_value, obs_error, obs_location, patch_obs, cotangent):
    obs_values = obs_value[0]
    obs_errors = obs_error[0]
    obs_cells = obs_location[0]
    patch_lists = patch_obs[0]
    current = initial_ensemble
    step_count = 0
    first_pad = padded_rows(current)
    first_rate = tendency(first_pad)
    middle = current + time_step * first_rate
    second_pad = padded_rows(middle)
    second_rate = tendency(second_pad)
    trajectory = [(first_pad, second_pad)]
    current = current + 0.5 * time_step * (first_rate + second_rate)
    member_values = current.reshape(current.shape[0], -1)[:, obs_cells]
    obs_ens = lax.all_gather(member_values, "member", axis=0, tiled=True)
    fore_owned, cot_owned = (
        lax.all_to_all(current, "member", split_axis=3, concat_axis=0, tiled=True),
        lax.all_to_all(cotangent, "member", split_axis=3, concat_axis=0, tiled=True),
    )
    updated_owned, grad_owned, obs_total = owner_update(
        fore_owned, cot_owned, obs_ens, obs_values, obs_errors, obs_cells, patch_lists
    )
    analysis, grad_state = (
        lax.all_to_all(updated_owned, "member", split_axis=0, concat_axis=3, tiled=True),
        lax.all_to_all(grad_owned, "member", split_axis=0, concat_axis=3, tiled=True),
    )
    my_grad_obs = lax.psum_scatter(obs_total, "member", scatter_dimension=0, tiled=True)
    flat_grad = grad_state.reshape(grad_state.shape[0], -1).at[:, obs_cells].add(my_grad_obs)
    gradient = flat_grad.reshape(grad_state.shape)
    for step_count in reversed(range(STEPS)):
        first_pad, second_pad = trajectory[step_count]
        second_pull = jax.vjp(tendency, second_pad)[1]
        grad_middle = return_rims(second_pull(0.5 * time_step * gradient)[0])
        grad_first = 0.5 * time_step * gradient + time_step * grad_middle
        first_pull = jax.vjp(tendency, first_pad)[1]
        gradient = gradient + grad_middle + return_rims(first_pull(grad_first)[0])
    return (analysis, gradient)


LANES = 128
HALO = 8
OBS_PAD = 640


def dot_full(a, b, dims):
    return lax.dot_general(
        a, b, (dims, ((), ())), precision=highest, preferred_element_type=jnp.float32
    )


def analysis_kernel(
    cur_ref, seen_ref, cot_ref, w_ref, val_ref, ana_out, grad_out, seen_out,
    mats, cells, pairs, an, vecs, obs, x_ref, got_seen, ana_ref, grad_ref, part_ref,
    ana_got, grad_got, part_got, send_sem, recv_sem,
):
    members = x_ref.shape[0]
    variables = cot_ref.shape[1]
    count = lax.axis_size("member")
    local = members // count
    me = lax.axis_index("member")

    barrier = pltpu.get_barrier_semaphore()
    for s in range(1, count):
        pl.semaphore_signal(
            barrier,
            inc=1,
            device_id={"member": lax.rem(me + s, count)},
            device_id_type=pl.DeviceIdType.MESH,
        )
    pl.semaphore_wait(barrier, count - 1)

    def lanes(ref, m):
        return ref.at[:, :, :, pl.ds(pl.multiple_of(m * LANES, LANES), LANES)]

    def portion(ref, m):
        return ref.at[pl.ds(pl.multiple_of(m * local, local), local)]

    def send(stream, source, target):
        copies = []
        for s in range(1, count):
            peer = lax.rem(me + s, count)
            copy = pltpu.make_async_remote_copy(
                src_ref=source(peer),
                dst_ref=target,
                send_sem=send_sem.at[stream, s - 1],
                recv_sem=recv_sem.at[stream, s - 1],
                device_id={"member": peer},
                device_id_type=pl.DeviceIdType.MESH,
            )
            copy.start()
            copies.append(copy)
        return copies

    def arrive(copies):
        for copy in copies:
            copy.wait_recv()

    seen_sent = send(0, lambda m: seen_ref.at[m], portion(got_seen, me))
    cur_sent = send(1, lambda m: lanes(cur_ref, m), portion(x_ref, me))
    mine = pl.ds(pl.multiple_of(me * local, local), local)
    own = pl.ds(pl.multiple_of(me * LANES, LANES), LANES)
    got_seen[mine] = seen_ref[me]
    x_ref[mine] = cur_ref[:, :, :, own]
    norm = float(members - 1)
    square = members * members
    group = 4

    def patch_map(r):
        patch = lax.broadcasted_iota(jnp.int32, (LANES, LANES), 0)
        col = lax.broadcasted_iota(jnp.int32, (LANES, LANES), 1)
        hit = (patch // 4 == col // 4) & (patch % 4 == r)
        return jnp.where(hit, 1.0, 0.0).astype(jnp.float32)

    def rows_of(ref, i, size):
        return ref[pl.ds(pl.multiple_of(i * size, size), size), :]

    def eye_row(i):
        at = lax.broadcasted_iota(jnp.int32, (members, LANES), 0)
        return jnp.where(at == i, 1.0, 0.0).astype(jnp.float32)

    def product(out, terms, scale=1.0, shift=0.0):
        def body(block, carry):
            base = pl.multiple_of(block * (group * members), group * members)
            totals = [jnp.zeros((members, LANES), jnp.float32) for _ in range(group)]
            for k in range(members):
                for a, b in terms:
                    right = mats[b, k * members : (k + 1) * members, :]
                    for g in range(group):
                        left = mats[a, pl.ds(base + g * members + k, 1), :]
                        totals[g] = totals[g] + left * right
            for g in range(group):
                done = totals[g]
                if scale != 1.0:
                    done = scale * done
                if shift != 0.0:
                    done = done + shift * eye_row(block * group + g)
                mats[out, pl.ds(base + g * members, members), :] = done
            return carry

        lax.fori_loop(0, members // group, body, 0)

    def times_vec(m, slot):
        total = jnp.zeros((members, LANES), jnp.float32)
        for k in range(members):
            total = total + mats[m, k * members : (k + 1) * members, :] * vecs[slot, k : k + 1, :]
        return total

    WB, B, M0, Y1, M1, Y2, Z2, M2, Y3, Z3, M3, Z4 = range(12)
    G, DM0, DY1, DM1, DY2, DZ2, DM2, DY3, DZ3, DM3, DZ4 = range(12, 23)

    arrive(seen_sent)
    for q in range(OBS_PAD // LANES):
        obs[:, q * LANES : (q + 1) * LANES] = got_seen[:, q, :]
    seen = obs[...]
    seen_mean = jnp.sum(seen, axis=0, keepdims=True) * (1.0 / members)
    spread = seen - seen_mean
    obs[...] = spread
    innovation = val_ref[...] - seen_mean

    def outer(k, carry):
        pairs[pl.ds(pl.multiple_of(k * members, members), members), :] = obs[pl.ds(k, 1), :] * spread
        return carry

    lax.fori_loop(0, members, outer, 0)
    weight = w_ref[...]
    mats[B] = dot_full(pairs[...], weight, ((1,), (0,)))
    forcing = dot_full(spread * innovation, weight, ((1,), (0,)))

    def add_eye(i, total):
        row = mats[B, pl.ds(pl.multiple_of(i * members, members), members), :] + norm * eye_row(i)
        mats[B, pl.ds(pl.multiple_of(i * members, members), members), :] = row
        return total + row * row

    energy = lax.fori_loop(0, members, add_eye, jnp.zeros((members, LANES), jnp.float32))
    scale = jnp.sqrt(jnp.sum(energy, axis=0, keepdims=True))
    inv = 1.0 / scale

    def normalise(i, carry):
        at = pl.ds(pl.multiple_of(i * members, members), members)
        row = mats[B, at, :] * inv
        mats[B, at, :] = row
        mats[M0, at, :] = 1.5 * eye_row(i) - 0.5 * row
        return carry

    lax.fori_loop(0, members, normalise, 0)
    product(Y1, [(B, M0)])
    product(M1, [(M0, Y1)], -0.5, 1.5)
    product(Y2, [(Y1, M1)])
    product(Z2, [(M1, M0)])
    product(M2, [(Z2, Y2)], -0.5, 1.5)
    product(Y3, [(Y2, M2)])
    product(Z3, [(M2, Z2)])
    product(M3, [(Z3, Y3)], -0.5, 1.5)
    product(Z4, [(M3, Z3)])

    vecs[0] = forcing
    half = times_vec(Z4, 0)
    vecs[1] = half
    mean_weight = times_vec(Z4, 1) * inv
    vecs[2] = mean_weight
    root = jnp.sqrt(norm) / jnp.sqrt(scale)

    arrive(cur_sent)
    xbar = lax.fori_loop(
        0, members, lambda k, t: t + x_ref[k], jnp.zeros((variables, 8, LANES), jnp.float32)
    ) * (1.0 / members)

    def centre(k, carry):
        an[k] = x_ref[k] - xbar
        return carry

    lax.fori_loop(0, members, centre, 0)

    for r in range(4):
        spread_r = dot_full(
            (
                mats[Z4].reshape(members, members, LANES) * root[None]
                + mean_weight[:, None, :]
            ).reshape(square, LANES),
            patch_map(r),
            ((1,), (0,)),
        )
        cells[pl.ds(2 * r, square, stride=8), :] = spread_r
        cells[pl.ds(2 * r + 1, square, stride=8), :] = spread_r

    def update(block, carry):
        totals = [xbar for _ in range(group)]
        for k in range(members):
            piece = an[k]
            for g in range(group):
                at = pl.multiple_of((block * group + g) * 8, 8)
                totals[g] = totals[g] + piece * cells[pl.ds(at + k * members * 8, 8), :][None]
        for g in range(group):
            ana_ref[block * group + g] = totals[g]
        return carry

    lax.fori_loop(0, members // group, update, 0)

    ana_sent = send(2, lambda m: portion(ana_ref, m), portion(ana_got, me))

    def pull(block, carry):
        zero = jnp.zeros((variables, 8, LANES), jnp.float32)
        totals = [zero for _ in range(group)]
        for j in range(members):
            piece = cot_ref[j]
            for g in range(group):
                at = pl.multiple_of((block * group + g) * members * 8, 8)
                totals[g] = totals[g] + piece * cells[pl.ds(at + j * 8, 8), :][None]
        for g in range(group):
            grad_ref[block * group + g] = totals[g]
            carry = carry - totals[g]
        return carry

    short = lax.fori_loop(0, members // group, pull, jnp.zeros((variables, 8, LANES), jnp.float32))
    short = lax.fori_loop(0, members, lambda j, t: t + cot_ref[j], short) * (1.0 / members)

    def settle(k, carry):
        grad_ref[k] = grad_ref[k] + short
        return carry

    lax.fori_loop(0, members, settle, 0)

    grad_sent = send(3, lambda m: portion(grad_ref, m), portion(grad_got, me))

    def cell_pair(block, carry):
        held = [an[block * group + g] for g in range(group)]
        for j in range(members):
            cot = cot_ref[j]
            for g in range(group):
                at = pl.multiple_of((block * group + g) * members * 8, 8)
                cells[pl.ds(at + j * 8, 8), :] = jnp.sum(held[g] * cot, axis=0)
        return carry

    lax.fori_loop(0, members // group, cell_pair, 0)
    cot_weights = jnp.zeros((square, LANES), jnp.float32)
    for r in range(4):
        both = cells[pl.ds(2 * r, square, stride=8), :] + cells[pl.ds(2 * r + 1, square, stride=8), :]
        cot_weights = cot_weights + dot_full(both, patch_map(r), ((1,), (1,)))
    mats[WB] = cot_weights

    cot_cube = mats[WB].reshape(members, members, LANES)
    mean_cot = jnp.sum(cot_cube, axis=1)
    vecs[3] = mean_cot
    half_cot = times_vec(Z4, 3) * inv
    vecs[4] = half_cot
    forcing_cot = times_vec(Z4, 4)
    overlap = jnp.sum(jnp.sum(mats[WB] * mats[Z4], axis=0, keepdims=True), axis=0, keepdims=True)
    scale_cot = (
        -0.5 * root * inv * overlap - jnp.sum(mean_cot * mean_weight, axis=0, keepdims=True) * inv
    )

    def symmetric(i, carry):
        at = pl.ds(pl.multiple_of(i * members, members), members)
        both = mats[WB, at, :] + mats[WB, pl.ds(i, members, stride=members), :]
        mean_i = vecs[3, pl.ds(i, 1), :]
        half_i = vecs[1, pl.ds(i, 1), :]
        half_cot_i = vecs[4, pl.ds(i, 1), :]
        forcing_i = vecs[0, pl.ds(i, 1), :]
        full = (0.5 * root) * both + 0.5 * (
            (mean_i * inv) * half
            + (half_i * inv) * mean_cot
            + half_cot_i * forcing
            + forcing_i * half_cot
        )
        mats[G, at, :] = full
        mats[DM0, at, :] = -0.5 * full
        return carry

    lax.fori_loop(0, members, symmetric, 0)
    product(DY1, [(G, M0), (B, DM0)])
    product(DM1, [(DM0, Y1), (M0, DY1)], -0.5)
    product(DY2, [(DY1, M1), (Y1, DM1)])
    product(DZ2, [(DM1, M0), (M1, DM0)])
    product(DM2, [(DZ2, Y2), (Z2, DY2)], -0.5)
    product(DY3, [(DY2, M2), (Y2, DM2)])
    product(DZ3, [(DM2, Z2), (M2, DZ2)])
    product(DM3, [(DZ3, Y3), (Z3, DY3)], -0.5)
    product(DZ4, [(DM3, Z3), (M3, DZ3)])
    scale_cot = scale_cot - jnp.sum(mats[DZ4] * mats[B], axis=0, keepdims=True) * inv
    gram_cot = mats[DZ4] * inv + scale_cot * mats[B]
    pairs[...] = dot_full(gram_cot, weight, ((1,), (1,)))
    scaled_cot = dot_full(forcing_cot, weight, ((1,), (1,)))
    seen_cot = scaled_cot * innovation

    def gather(j, total):
        block = pairs[pl.ds(pl.multiple_of(j * members, members), members), :]
        return total + block * obs[pl.ds(j, 1), :]

    seen_cot = seen_cot + 2.0 * lax.fori_loop(
        0, members, gather, jnp.zeros((members, OBS_PAD), jnp.float32)
    )
    innovation_cot = jnp.sum(scaled_cot * spread, axis=0, keepdims=True)
    mean_part = innovation_cot + jnp.sum(seen_cot, axis=0, keepdims=True)
    seen_cot = seen_cot - mean_part * (1.0 / members)
    for q in range(OBS_PAD // LANES):
        part_ref[:, q, :] = seen_cot[:, q * LANES : (q + 1) * LANES]
    for q in range(OBS_PAD // LANES, 8):
        part_ref[:, q, :] = jnp.zeros((members, LANES), jnp.float32)
    part_sent = send(4, lambda m: portion(part_ref, m), portion(part_got, me))
    ana_got[mine] = ana_ref[mine]
    grad_got[mine] = grad_ref[mine]
    part_got[mine] = part_ref[mine]
    arrive(ana_sent)
    arrive(grad_sent)
    for m in range(count):
        cut = slice(m * local, (m + 1) * local)
        ana_out[:, :, :, m * LANES : (m + 1) * LANES] = ana_got[cut]
        grad_out[:, :, :, m * LANES : (m + 1) * LANES] = grad_got[cut]
    arrive(part_sent)
    for m in range(count):
        seen_out[m] = part_got[m * local : (m + 1) * local]
    for copies in (seen_sent, cur_sent, ana_sent, grad_sent, part_sent):
        for copy in copies:
            copy.wait_send()


def analysis_call(current, seen, cotangent, weight, val):
    count = seen.shape[0]
    local, variables = current.shape[:2]
    members = count * local
    square = members * members
    whole = pltpu.VMEM((members, variables, 8, LANES), jnp.float32)
    small = pltpu.VMEM((members, 8, LANES), jnp.float32)
    scratch = [
        pltpu.VMEM((23, square, LANES), jnp.float32),
        pltpu.VMEM((square * 8, LANES), jnp.float32),
        pltpu.VMEM((square, OBS_PAD), jnp.float32),
        whole,
        pltpu.VMEM((5, members, LANES), jnp.float32),
        pltpu.VMEM((members, OBS_PAD), jnp.float32),
        whole,
        small,
        whole,
        whole,
        small,
        whole,
        whole,
        small,
        pltpu.SemaphoreType.DMA((5, count - 1)),
        pltpu.SemaphoreType.DMA((5, count - 1)),
    ]
    return pl.pallas_call(
        analysis_kernel,
        out_shape=(
            jax.ShapeDtypeStruct(current.shape, jnp.float32),
            jax.ShapeDtypeStruct(current.shape, jnp.float32),
            jax.ShapeDtypeStruct(seen.shape, jnp.float32),
        ),
        in_specs=[pl.BlockSpec(memory_space=pltpu.VMEM)] * 5,
        out_specs=(pl.BlockSpec(memory_space=pltpu.VMEM),) * 3,
        scratch_shapes=scratch,
        compiler_params=pltpu.CompilerParams(
            vmem_limit_bytes=56 * 2**20, collective_id=0, has_side_effects=True
        ),
    )(current, seen, cotangent, weight, val)


def by_slot(flat, per_col):
    return flat.reshape(-1, per_col).T


def wrapped(rows):
    return jnp.concatenate([rows[..., -HALO:], rows, rows[..., :HALO]], axis=-1)


def obs_weights(obs_values, obs_errors, obs_cells, patch_lists, columns, tile_rows):
    nobs = obs_values.shape[0]
    per_col = nobs // MESH_WIDTH
    first_col = lax.axis_index("member") * columns
    span = columns + 2 * HALO

    def window(flat, fill):
        rows = wrapped(by_slot(flat, per_col))
        cut = lax.dynamic_slice_in_dim(rows, first_col, span, 1).reshape(-1)
        return jnp.pad(cut, (0, OBS_PAD - per_col * span), constant_values=fill)

    ids = window(jnp.arange(nobs, dtype=jnp.int32), -1)[:, None]
    located = window(obs_cells, 0)[:, None]
    errors = window(obs_errors, 1.0)[:, None]
    values = window(obs_values, 0.0)[None]
    half_rows = tile_rows // 2
    patch_ids = jnp.arange(patch_lists.shape[0], dtype=jnp.int32)[None]
    patch_col = patch_ids // half_rows
    patch_row = patch_ids % half_rows
    times = jnp.sum((patch_lists.T[:, None, :] == ids[None]).astype(jnp.float32), axis=0)
    obs_row = located // MESH_WIDTH % tile_rows
    obs_col = located % MESH_WIDTH
    row_gap = (obs_row - 2 * patch_row).astype(jnp.float32) - 0.5
    col_shift = obs_col - 4 * patch_col - first_col
    col_shift = (col_shift + MESH_WIDTH // 2) % MESH_WIDTH - MESH_WIDTH // 2
    col_gap = col_shift.astype(jnp.float32) - 1.5
    weight = times * (
        jnp.exp(-(row_gap * row_gap + col_gap * col_gap) / (2.0 * LOC_R * LOC_R)) / errors
    )
    return weight, values


def shards(initial_ensemble, obs_value, obs_error, obs_location, patch_obs, cotangent):
    obs_values = obs_value[0]
    obs_errors = obs_error[0]
    obs_cells = obs_location[0]
    patch_lists = patch_obs[0]
    count = lax.axis_size("member")
    local, variables, tile_rows, width = initial_ensemble.shape
    columns = width // count
    per_col = obs_cells.shape[0] // width
    span = columns + 2 * HALO
    stacked = variables * tile_rows

    parts = jnp.stack([cotangent[..., m * columns : (m + 1) * columns] for m in range(count)])
    cot_owned = lax.all_to_all(parts, "member", split_axis=0, concat_axis=0, tiled=True)
    cot_owned = cot_owned.reshape(count * local, variables, tile_rows, columns)
    weight, values = obs_weights(obs_values, obs_errors, obs_cells, patch_lists, columns, tile_rows)
    current = initial_ensemble
    first_pad = padded_rows(current)
    first_rate = tendency(first_pad)
    middle = current + time_step * first_rate
    second_pad = padded_rows(middle)
    second_rate = tendency(second_pad)
    current = current + 0.5 * time_step * (first_rate + second_rate)

    slot_cells = by_slot(obs_cells // width, per_col)
    level = jnp.arange(stacked, dtype=jnp.int32)[:, None]
    masks = [level == slot_cells[i][None] for i in range(per_col)]
    flat = current.reshape(local, stacked, width)
    seen = jnp.stack([jnp.sum(jnp.where(m, flat, 0.0), axis=1) for m in masks], axis=1)
    seen = wrapped(seen)
    seen = jnp.stack(
        [seen[..., m * columns : m * columns + span].reshape(local, per_col * span) for m in range(count)]
    )
    seen = jnp.pad(seen, ((0, 0), (0, 0), (0, tile_rows * LANES - per_col * span)))
    seen = seen.reshape(count, local, tile_rows, LANES)
    analysis, grad_state, back = analysis_call(current, seen, cot_owned, weight, values)
    seen_back = back.reshape(count, local, -1)[..., : per_col * span]
    seen_back = seen_back.reshape(count, local, per_col, span)
    total = sum(
        jnp.pad(seen_back[m], ((0, 0), (0, 0), (m * columns, width - columns - m * columns)))
        for m in range(count)
    )
    core = total[..., HALO:-HALO]
    head = total[..., -HALO:]
    tail = total[..., :HALO]
    core = core + jnp.concatenate(
        [head, jnp.zeros(core.shape[:-1] + (width - 2 * HALO,), jnp.float32), tail], axis=-1
    )
    gradient = grad_state.reshape(local, stacked, width)
    for i in range(per_col):
        gradient = gradient + jnp.where(masks[i], core[:, i][:, None], 0.0)
    gradient = gradient.reshape(initial_ensemble.shape)
    second_pull = jax.vjp(tendency, second_pad)[1]
    grad_middle = return_rims(second_pull(0.5 * time_step * gradient)[0])
    grad_first = 0.5 * time_step * gradient + time_step * grad_middle
    first_pull = jax.vjp(tendency, first_pad)[1]
    gradient = gradient + grad_middle + return_rims(first_pull(grad_first)[0])
    return (analysis, gradient)


def fits(initial_ensemble, obs_value, obs_error, obs_location, patch_obs, cotangent):
    members = initial_ensemble.shape[0] * lax.axis_size("member")
    width = initial_ensemble.shape[3]
    columns = width // lax.axis_size("member")
    nobs = obs_location.shape[1]
    return (
        members <= 32
        and columns == LANES
        and initial_ensemble.shape[2] == 8
        and nobs % width == 0
        and patch_obs.shape[2] // 2 <= 8 * nobs // width
        and nobs // width * (columns + 2 * HALO) <= OBS_PAD
    )


def chosen(*args):
    return shards(*args) if fits(*args) else shards_wide(*args)


def solution(mesh):
    placed = (
        P("member", None, "space", None),
        P("space", None),
        P("space", None),
        P("space", None),
        P("space", "member", None),
        P("member", None, "space", None),
    )
    return jax.shard_map(
        chosen,
        mesh=mesh,
        in_specs=placed,
        out_specs=(P("member", None, "space", None), P("member", None, "space", None)),
        check_vma=False,
    )
```
